32 devices in a mesh: groups: 2 (over x), seq: 8 (over z, y), tensor: 2 (over core).
Axes of the slice: x: 2, y: 2, z: 4, core: 2. Of those that a mesh axis runs over, the one named last changes fastest.
Arguments:
- inputs: bfloat16 [4096, 1536], P(('groups', 'seq'), 'tensor'), parts along dimension 0, may hold values from -6 to 6
- w_dilated: bfloat16 [1536, 3, 1536], P(None, None, 'tensor'), may hold values from -0.09375 to 0.09375
- w_point: bfloat16 [1536, 1536], P(None, 'tensor'), may hold values from -0.15625 to 0.15625
- cotangent: bfloat16 [4096, 1536], P(('groups', 'seq'), 'tensor'), parts along dimension 0, may hold values from -6 to 6
Outputs:
- output: bfloat16 [4096, 1536], P(('groups', 'seq'), 'tensor'), parts along dimension 0
- grad_inputs: bfloat16 [4096, 1536], P(('groups', 'seq'), 'tensor'), parts along dimension 0
- grad_point: float32 [3072, 1536], P(('groups', 'seq'), 'tensor'), parts along dimension 0
The draws below stay inside these ranges and needn't reach their ends.
There are 2 independent parts, one for each index of `groups`. The reference program is written for one: setup_inputs(seed, part) draws one part's arguments, and reference() takes and returns one part's arrays. A program takes and returns all parts, laid end to end along the dimension named above; an argument that names none is the same for every part. Nothing has to cross between parts.
All inputs are finite; a program needn't handle non-finite values.
Results may differ from the reference program's by a relative error of at most 0.007.
Values may be sent and summed in bfloat16 or wider, within the bound.
A program may use at most 64 MiB of HBM per device.

```python
import math
import jax
import jax.numpy as jnp

C = 1536
DILATION_BINS = 32
TOTAL_BINS = 2048
N_TENSOR = 2


def spiked(drawn, own_key, source, target, blocks, factor):
    def block_of(axis_at):
        return (jnp.arange(drawn.shape[axis_at]) // (drawn.shape[axis_at] // blocks)).reshape((-1,) + (1,) * (drawn.ndim - 1 - axis_at))

    one_side = jax.random.permutation(own_key, blocks)[block_of(target)]
    other_side = (block_of(target) + blocks // 2) % blocks
    return jnp.where((block_of(source) == one_side) | (block_of(source) == other_side), factor * drawn, drawn)


def levels(key, dims, shards, low, largest):
    level = 1.0
    for axis_at, blocks in shards:
        heights = jax.random.uniform(jax.random.fold_in(jax.random.fold_in(key, 6), axis_at), (blocks,), jnp.float32, low / len(shards), largest / len(shards))
        level = level * jnp.repeat(jnp.exp(heights), dims[axis_at] // blocks).reshape((-1,) + (1,) * (len(dims) - 1 - axis_at))
    return level


def normal_values(own_key, extent, width, reach, split=(), dtype=jnp.bfloat16):
    values = width * jax.random.normal(own_key, extent, jnp.float32)
    if split:
        values = values * levels(own_key, extent, split, -0.22, 0.18)
    return jnp.clip(values, -reach, reach).astype(dtype)


def gaussian_with(key, shape, scale, reach, shards, heavy, kind=jnp.bfloat16):
    drawn = scale * jax.random.normal(key, shape, jnp.float32)
    if shards:
        drawn = drawn * levels(key, shape, shards, -0.22, 0.18)
    return jnp.clip(spiked(drawn, jax.random.fold_in(key, 3), *heavy), -reach, reach).astype(kind)


def setup_inputs(seed: int = 0, part: int = 0) -> dict:
    seeds = jax.random.split(jax.random.key(seed), 5)
    part_keys = jax.random.split(jax.random.fold_in(seeds[4], part), 5)
    inputs = gaussian_with(part_keys[0], (TOTAL_BINS, C), 1.0, 6.0, ((0, 8), (1, 2)), (0, 1, 8, 2.0))
    w_dilated = normal_values(seeds[1], (C, 3, C), (3 * C) ** -0.5, 0.09375, ((2, 2),))
    w_point = normal_values(seeds[2], (C, C), C ** -0.5, 0.15625, ((1, 2),))
    cotangent = gaussian_with(part_keys[3], (TOTAL_BINS, C), 1.0, 6.0, ((0, 8), (1, 2)), (0, 1, 8, 2.0))
    return {"inputs": inputs, "w_dilated": w_dilated, "w_point": w_point, "cotangent": cotangent}


gelu_cubic = 0.044715
gelu_scale = math.sqrt(2.0 / math.pi)

def gelu_pair(values):
    inner = gelu_scale * (values + gelu_cubic * values * values * values)
    tangent = jnp.tanh(inner)
    result = 0.5 * values * (1.0 + tangent)
    derivative = 0.5 * (1.0 + tangent) + 0.5 * values * (1.0 - tangent * tangent) * gelu_scale * (1.0 + 3.0 * gelu_cubic * values * values)
    return (result, derivative)

def reference(inputs, w_dilated, w_point, cotangent):
    length_bins = inputs.shape[0]
    group_width = C // N_TENSOR
    padded_input = jnp.pad(inputs, ((DILATION_BINS, DILATION_BINS), (0, 0)))
    displaced_rows = [padded_input[kernel_tap_index * DILATION_BINS:kernel_tap_index * DILATION_BINS + length_bins] for kernel_tap_index in range(3)]
    hidden = jnp.dot(displaced_rows[0], w_dilated[:, 0, :], preferred_element_type=jnp.float32)
    hidden = hidden + jnp.dot(displaced_rows[1], w_dilated[:, 1, :], preferred_element_type=jnp.float32)
    hidden = hidden + jnp.dot(displaced_rows[2], w_dilated[:, 2, :], preferred_element_type=jnp.float32)
    activation, derivative = gelu_pair(hidden)
    activation = activation.astype(jnp.bfloat16)
    mixed_sum = inputs.astype(jnp.float32)
    for group_index in range(N_TENSOR):
        lower = group_index * group_width
        part_sum = jnp.dot(activation[:, lower:lower + group_width], w_point[:, lower:lower + group_width].T, preferred_element_type=jnp.float32)
        mixed_sum = mixed_sum + part_sum.astype(jnp.bfloat16).astype(jnp.float32)
    output = mixed_sum.astype(jnp.bfloat16)
    grad_act = jnp.dot(cotangent, w_point, preferred_element_type=jnp.float32)
    hidden_gradient = (grad_act * derivative).astype(jnp.bfloat16)
    grad_point = jnp.dot(cotangent.T, activation, preferred_element_type=jnp.float32)
    padded_gradient = jnp.pad(hidden_gradient, ((DILATION_BINS, DILATION_BINS), (0, 0)))
    back_sum = cotangent.astype(jnp.float32)
    for group_index in range(N_TENSOR):
        lower = group_index * group_width
        part_sum = jnp.zeros((length_bins, C), jnp.float32)
        for kernel_tap_index in range(3):
            anchor_position = (2 - kernel_tap_index) * DILATION_BINS
            part_sum = part_sum + jnp.dot(padded_gradient[anchor_position:anchor_position + length_bins, lower:lower + group_width], w_dilated[:, kernel_tap_index, lower:lower + group_width].T, preferred_element_type=jnp.float32)
        back_sum = back_sum + part_sum.astype(jnp.bfloat16).astype(jnp.float32)
    grad_inputs = back_sum.astype(jnp.bfloat16)
    return (output, grad_inputs, grad_point)
```

```python
import functools
import math

import jax
import jax.numpy as jnp
from jax import lax
from jax.experimental import pallas as pl
from jax.experimental.pallas import tpu as pltpu
from jax.sharding import PartitionSpec as P

DILATION_BINS = 32
MESH = pl.DeviceIdType.MESH

gelu_cubic = 0.044715
gelu_scale = math.sqrt(2.0 / math.pi)


def gelu_pair(values):
    square = values * values
    tangent = jnp.tanh(gelu_scale * (values + gelu_cubic * square * values))
    half = 0.5 * (1.0 + tangent)
    slope = half + 0.5 * values * (1.0 - tangent * tangent) * gelu_scale * (
        1.0 + 3.0 * gelu_cubic * square
    )
    return values * half, slope


def dot_nn(a, b):
    return jnp.dot(a, b, preferred_element_type=jnp.float32)


def dot_nt(a, b):
    return lax.dot_general(a, b, (((1,), (1,)), ((), ())), preferred_element_type=jnp.float32)


def kernel(n, tile, with_point, *refs):
    x_ref, w_hbm, p_hbm, d_ref = refs[:4]
    if with_point:
        out_ref, gi_ref, gp_ref = refs[4:7]
        act, dfull = refs[7:9]
        rest = refs[9:]
    else:
        out_ref, gi_ref, act, dfull = refs[4:8]
        rest = refs[8:]
    (w, p, xfull, slope, ghpad, msend, mrecv, bsend, brecv) = rest[:9]
    (lsem, ssem, rsem, xs_sem, xr_sem, gs_sem, gr_sem) = rest[9:16]
    if with_point:
        (actp, dp, dps, cot_t, gps, gpr, as_sem, ar_sem, ps_sem, pr_sem) = rest[16:]

    s = lax.axis_index("seq")
    t = lax.axis_index("tensor")
    o = 1 - t
    T, H = x_ref.shape
    C = 2 * H
    R = DILATION_BINS
    tiles = H // tile
    bf16 = jnp.bfloat16
    has_low = s > 0
    has_high = s < n - 1
    mine = pl.ds(pl.multiple_of(t * H, H), H)
    other = pl.ds(pl.multiple_of(o * H, H), H)
    nz = n // 2
    z = s // 2
    y = lax.rem(s, 2)
    pair = s + 1 - 2 * y

    def remote(src, dst, send, recv, seq, tensor):
        return pltpu.make_async_remote_copy(
            src_ref=src,
            dst_ref=dst,
            send_sem=send,
            recv_sem=recv,
            device_id={"seq": seq, "tensor": tensor},
            device_id_type=MESH,
        )

    def cols(j):
        return pl.ds(pl.multiple_of(j * tile, tile), tile)

    w_loads = [pltpu.make_async_copy(w_hbm.at[k], w.at[k], lsem.at[k]) for k in range(3)]
    p_load = pltpu.make_async_copy(p_hbm, p, lsem.at[3])
    for load in w_loads:
        load.start()
    p_load.start()

    barrier = pltpu.get_barrier_semaphore()

    def greet(seq, tensor):
        pl.semaphore_signal(
            barrier, inc=1, device_id={"seq": seq, "tensor": tensor}, device_id_type=MESH
        )

    greet(s, o)

    @pl.when(has_low)
    def _():
        greet(s - 1, t)
        greet(s - 1, o)

    @pl.when(has_high)
    def _():
        greet(s + 1, t)
        greet(s + 1, o)

    if with_point:
        for d in range(1, nz):
            greet(lax.rem(z + d, nz) * 2 + y, t)
    xfull[pl.ds(R, T), mine] = x_ref[...]
    dfull[:, mine] = d_ref[...]
    sides = lax.div(s + n - 1, n) + lax.div(2 * n - 2 - s, n)
    pl.semaphore_wait(barrier, 1 + (nz - 1 if with_point else 0) + 2 * sides)

    def to_low(slot, tensor):
        return remote(
            x_ref.at[pl.ds(0, R), :], xfull.at[pl.ds(R + T, R), mine],
            xs_sem.at[slot], xr_sem.at[2 + t], s - 1, tensor,
        )

    def to_high(slot, tensor):
        return remote(
            x_ref.at[pl.ds(T - R, R), :], xfull.at[pl.ds(0, R), mine],
            xs_sem.at[2 + slot], xr_sem.at[t], s + 1, tensor,
        )

    @pl.when(has_low)
    def _():
        to_low(0, t).start()
        to_low(1, o).start()

    @pl.when(has_high)
    def _():
        to_high(0, t).start()
        to_high(1, o).start()

    x_side = remote(x_ref, xfull.at[pl.ds(R, T), mine], ssem.at[0], rsem.at[0], s, o)
    x_side.start()
    d_side = remote(d_ref, dfull.at[:, mine], ssem.at[1], rsem.at[1], s, o)
    d_side.start()
    if with_point:
        d_pair = remote(d_ref, dp, ssem.at[2], rsem.at[2], pair, t)
        d_pair.start()
        d_next = remote(dp, dps, ssem.at[3], rsem.at[3], s, o)
        cot_t[mine, pl.ds(0, T)] = d_ref[...].T

    @pl.when(s == 0)
    def _():
        xfull[pl.ds(0, R), :] = jnp.zeros((R, C), bf16)
        ghpad[pl.ds(0, R), :] = jnp.zeros((R, H), bf16)

    @pl.when(s == n - 1)
    def _():
        xfull[pl.ds(R + T, R), :] = jnp.zeros((R, C), bf16)
        ghpad[pl.ds(R + T, R), :] = jnp.zeros((R, H), bf16)

    remote(x_ref, xfull.at[pl.ds(R, T), other], ssem.at[0], rsem.at[0], s, o).wait_recv()

    @pl.when(has_low)
    def _():
        for half in range(2):
            remote(
                x_ref.at[pl.ds(0, R), :], xfull.at[pl.ds(0, R), pl.ds(half * H, H)],
                xs_sem.at[0], xr_sem.at[half], s - 1, t,
            ).wait_recv()

    @pl.when(has_high)
    def _():
        for half in range(2):
            remote(
                x_ref.at[pl.ds(0, R), :], xfull.at[pl.ds(R + T, R), pl.ds(half * H, H)],
                xs_sem.at[0], xr_sem.at[2 + half], s + 1, t,
            ).wait_recv()

    for load in w_loads:
        load.wait()

    def act_copy(j):
        return remote(
            act.at[j], actp.at[j], as_sem.at[j], ar_sem.at[j], pair, t
        )

    @pl.loop(0, tiles)
    def _(j):
        hidden = dot_nn(xfull[pl.ds(0, T), :], w[0, :, cols(j)])
        hidden += dot_nn(xfull[pl.ds(R, T), :], w[1, :, cols(j)])
        hidden += dot_nn(xfull[pl.ds(2 * R, T), :], w[2, :, cols(j)])
        value, derivative = gelu_pair(hidden)
        act[j] = value.astype(bf16)
        slope[:, cols(j)] = derivative
        if with_point:
            act_copy(j).start()

    if with_point:
        remote(d_ref, dp, ssem.at[2], rsem.at[2], pair, t).wait_recv()
        d_next.start()
        cot_t[mine, pl.ds(T, T)] = dp[...].T
    remote(d_ref, dfull.at[:, other], ssem.at[1], rsem.at[1], s, o).wait_recv()
    p_load.wait()
    if with_point:
        cot_t[other, pl.ds(0, T)] = dfull[:, other].T

    @pl.loop(0, tiles)
    def _(j):
        grad = dot_nn(dfull[...], p[:, cols(j)]) * slope[:, cols(j)]
        ghpad[pl.ds(R, T), cols(j)] = grad.astype(bf16)

    gh_low = remote(
        ghpad.at[pl.ds(R, R), :], ghpad.at[pl.ds(R + T, R), :],
        gs_sem.at[0], gr_sem.at[1], s - 1, t,
    )
    gh_high = remote(
        ghpad.at[pl.ds(T, R), :], ghpad.at[pl.ds(0, R), :],
        gs_sem.at[1], gr_sem.at[0], s + 1, t,
    )

    @pl.when(has_low)
    def _():
        gh_low.start()

    @pl.when(has_high)
    def _():
        gh_high.start()

    def point_copy(d, j):
        return remote(
            gps.at[d - 1, j], gpr.at[d - 1, j], ps_sem.at[d - 1, j], pr_sem.at[d - 1, j],
            lax.rem(z + d, nz) * 2 + y, t,
        )

    if with_point:
        rows = gp_ref.shape[0]
        remote(dp, dps, ssem.at[3], rsem.at[3], s, o).wait_recv()
        cot_t[other, pl.ds(T, T)] = dps[...].T

        @pl.loop(0, tiles)
        def _(j):
            act_copy(j).wait_recv()

            def block(d):
                owner = lax.rem(z + d, nz) * 2 + y
                at = pl.ds(pl.multiple_of(owner * rows, rows), rows)
                return dot_nn(cot_t[at, pl.ds(0, T)], act[j]) + dot_nn(
                    cot_t[at, pl.ds(T, T)], actp[j]
                )

            for d in range(1, nz):
                gps[d - 1, j] = block(d).astype(bf16)
                point_copy(d, j).start()
            gp_ref[:, cols(j)] = block(0)

    def mixed(at):
        total = dot_nt(act[0], p[at, pl.ds(0, tile)])
        for i in range(1, tiles):
            total += dot_nt(act[i], p[at, pl.ds(i * tile, tile)])
        return total.astype(bf16)

    @pl.loop(0, tiles)
    def _(j):
        msend[:, cols(j)] = mixed(pl.ds(pl.multiple_of(o * H + j * tile, tile), tile))

    m_side = remote(msend, mrecv, ssem.at[4], rsem.at[4], s, o)
    m_side.start()

    @pl.when(has_low)
    def _():
        remote(
            ghpad.at[pl.ds(R, R), :], ghpad.at[pl.ds(0, R), :],
            gs_sem.at[0], gr_sem.at[0], s - 1, t,
        ).wait_recv()

    @pl.when(has_high)
    def _():
        remote(
            ghpad.at[pl.ds(R, R), :], ghpad.at[pl.ds(R + T, R), :],
            gs_sem.at[0], gr_sem.at[1], s + 1, t,
        ).wait_recv()

    def back(at):
        total = dot_nt(ghpad[pl.ds(2 * R, T), :], w[0, at, :])
        total += dot_nt(ghpad[pl.ds(R, T), :], w[1, at, :])
        total += dot_nt(ghpad[pl.ds(0, T), :], w[2, at, :])
        return total.astype(bf16)

    @pl.loop(0, tiles)
    def _(j):
        bsend[:, cols(j)] = back(pl.ds(pl.multiple_of(o * H + j * tile, tile), tile))

    b_side = remote(bsend, brecv, ssem.at[5], rsem.at[5], s, o)
    b_side.start()
    m_side.wait_recv()

    @pl.loop(0, tiles)
    def _(j):
        own = mixed(pl.ds(pl.multiple_of(t * H + j * tile, tile), tile))
        total = x_ref[:, cols(j)].astype(jnp.float32) + own.astype(jnp.float32)
        out_ref[:, cols(j)] = (total + mrecv[:, cols(j)].astype(jnp.float32)).astype(bf16)

    b_side.wait_recv()

    @pl.loop(0, tiles)
    def _(j):
        own = back(pl.ds(pl.multiple_of(t * H + j * tile, tile), tile))
        total = d_ref[:, cols(j)].astype(jnp.float32) + own.astype(jnp.float32)
        gi_ref[:, cols(j)] = (total + brecv[:, cols(j)].astype(jnp.float32)).astype(bf16)

    if with_point:

        @pl.loop(0, tiles)
        def _(j):
            total = gp_ref[:, cols(j)]
            for d in range(1, nz):
                point_copy(d, j).wait_recv()
                total += gpr[d - 1, j].astype(jnp.float32)
            gp_ref[:, cols(j)] = total

    @pl.when(has_low)
    def _():
        to_low(0, t).wait_send()
        to_low(1, o).wait_send()
        gh_low.wait_send()

    @pl.when(has_high)
    def _():
        to_high(0, t).wait_send()
        to_high(1, o).wait_send()
        gh_high.wait_send()

    x_side.wait_send()
    d_side.wait_send()
    m_side.wait_send()
    b_side.wait_send()
    if with_point:
        d_pair.wait_send()
        d_next.wait_send()

        @pl.loop(0, tiles)
        def _(j):
            act_copy(j).wait_send()
            for d in range(1, nz):
                point_copy(d, j).wait_send()


def kernel8(tile, *refs):
    x_hbm, w_hbm, p_hbm, d_hbm, out_ref, gi_ref, gp_ref = refs[:7]
    (w, p, xpad, rim, hid, slope, act, actp, d, dt, ct, ghpad) = refs[7:19]
    (msend, mrecv, bsend, brecv, gps, gpa, gpb) = refs[19:26]
    (load, x_s, x_r, d_s, d_r, rim_s, rim_r, rimf_s, rimf_r, co_s, co_r) = refs[26:37]
    (cp_s, cp_r, cf_s, cf_r, a_s, a_r, gh_s, gh_r, m_s, m_r, b_s, b_r) = refs[37:49]
    (z_s, za_r, zb_r) = refs[49:]

    s = lax.axis_index("seq")
    t = lax.axis_index("tensor")
    o = 1 - t
    z = s // 2
    y = lax.rem(s, 2)
    pair = s + 1 - 2 * y
    T, H = out_ref.shape
    R = DILATION_BINS
    rows = gp_ref.shape[0]
    tiles = H // tile
    chunks, wide = act.shape[0], act.shape[2]
    per = tile // wide
    bf16, f32 = jnp.bfloat16, jnp.float32
    low = s > 0
    high = s < 7
    outer = lax.rem(z + 1, 4) < 2
    inner = lax.rem(z + 1, 4) >= 2
    upper = z // 2
    far_outer = 3 - 3 * upper
    far_inner = 2 - upper
    near_inner = 1 + upper
    near_outer = 3 * upper
    early = 1 - upper

    def remote(src, dst, send, recv, seq, tensor):
        return pltpu.make_async_remote_copy(
            src_ref=src, dst_ref=dst, send_sem=send, recv_sem=recv,
            device_id={"seq": seq, "tensor": tensor}, device_id_type=MESH,
        )

    def cols(j):
        return pl.ds(pl.multiple_of(j * tile, tile), tile)

    barrier = pltpu.get_barrier_semaphore()

    def greet(seq, tensor):
        pl.semaphore_signal(
            barrier, inc=1, device_id={"seq": seq, "tensor": tensor}, device_id_type=MESH
        )

    greet(pair, t)

    @pl.when(z > 0)
    def _():
        greet(s - 2, t)

    @pl.when(z < 3)
    def _():
        greet(s + 2, t)

    @pl.when(jnp.logical_and(y == 0, z > 0))
    def _():
        greet(s - 1, t)

    @pl.when(jnp.logical_and(y == 1, z < 3))
    def _():
        greet(s + 1, t)

    greet(s, o)

    own = pl.ds(pl.multiple_of(t * H, H), H)
    other = pl.ds(pl.multiple_of(o * H, H), H)
    body = pl.ds(R, T)
    x_load = pltpu.make_async_copy(x_hbm, xpad.at[t, body], load.at[0])
    d_load = pltpu.make_async_copy(d_hbm, d.at[t], load.at[1])
    w_own = [
        pltpu.make_async_copy(w_hbm.at[k, own], w.at[k, own], load.at[2 + k]) for k in range(3)
    ]
    w_other = [
        pltpu.make_async_copy(w_hbm.at[k, other], w.at[k, other], load.at[5 + k])
        for k in range(3)
    ]
    p_load = pltpu.make_async_copy(p_hbm, p, load.at[8])
    for copy in [d_load, x_load] + w_own + w_other + [p_load]:
        copy.start()

    for half in range(2):
        xpad[half, pl.ds(0, R)] = jnp.zeros((R, H), bf16)
        xpad[half, pl.ds(R + T, R)] = jnp.zeros((R, H), bf16)

    @pl.when(s == 0)
    def _():
        rim[0] = jnp.zeros((2, R, H), bf16)
        ghpad[pl.ds(0, R), :] = jnp.zeros((R, H), bf16)

    @pl.when(s == 7)
    def _():
        rim[1] = jnp.zeros((2, R, H), bf16)
        ghpad[pl.ds(R + T, R), :] = jnp.zeros((R, H), bf16)

    d_load.wait()
    dt[...] = d[t].T

    def dt_block(i, side):
        return pl.ds(pl.multiple_of((2 * i + side) * rows, rows), rows)

    for i in range(2):
        ct[2 * t + i, 0] = dt[dt_block(i, y), :]

    x_load.wait()
    for copy in w_own:
        copy.wait()

    def taps(half, rows_of, j):
        total = dot_nn(xpad[half, pl.ds(0, T)], w[0, rows_of, cols(j)])
        total += dot_nn(xpad[half, pl.ds(R, T)], w[1, rows_of, cols(j)])
        return total + dot_nn(xpad[half, pl.ds(2 * R, T)], w[2, rows_of, cols(j)])

    @pl.loop(0, tiles)
    def _(j):
        hid[:, cols(j)] = taps(t, own, j)

    met = 2 + jnp.where(z > 0, 1, 0) + jnp.where(z < 3, 1, 0)
    pl.semaphore_wait(barrier, met + jnp.where(jnp.where(y == 0, z > 0, z < 3), 1, 0))

    to_low = remote(
        xpad.at[t, pl.ds(R, R)], rim.at[1, t], rim_s.at[0], rim_r.at[1], s - 1, t
    )
    to_high = remote(
        xpad.at[t, pl.ds(T, R)], rim.at[0, t], rim_s.at[1], rim_r.at[0], s + 1, t
    )

    def when_low(act_on):
        pl.when(low)(act_on)

    def when_high(act_on):
        pl.when(high)(act_on)

    when_low(to_low.start)
    when_high(to_high.start)
    x_side = remote(xpad.at[t, body], xpad.at[t, body], x_s, x_r, s, o)
    x_side.start()

    cot_pair = [
        remote(dt.at[dt_block(i, 1 - y), :], ct.at[2 * t + i, 1], cp_s.at[i], cp_r.at[i], pair, t)
        for i in range(2)
    ]
    cot_on = [
        remote(ct.at[2 * t + i, 1], ct.at[2 * t + i, 1], cf_s.at[i], cf_r.at[i], s, o)
        for i in range(2)
    ]
    cot_own = [
        remote(ct.at[2 * t + i, 0], ct.at[2 * t + i, 0], co_s.at[i], co_r.at[i], s, o)
        for i in range(2)
    ]

    def each(copies, what):
        def run():
            for copy in copies:
                getattr(copy, what)()
        return run

    pl.when(t == early)(each(cot_pair, "start"))
    d_side = remote(d.at[t], d.at[t], d_s, d_r, s, o)
    d_side.start()
    each(cot_own, "start")()

    remote(xpad.at[t, body], xpad.at[o, body], x_s, x_r, s, o).wait_recv()
    for copy in w_other:
        copy.wait()

    @pl.loop(0, tiles)
    def _(j):
        hid[:, cols(j)] += taps(o, other, j)

    def rim_on(k):
        return remote(rim.at[k, t], rim.at[k, t], rimf_s.at[k], rimf_r.at[k], s, o)

    def rim_land(k):
        remote(xpad.at[t, pl.ds(R, R)], rim.at[k, t], rim_s.at[0], rim_r.at[k], s, o).wait_recv()
        rim_on(k).start()

    def rim_land_on(k):
        remote(rim.at[k, t], rim.at[k, o], rimf_s.at[k], rimf_r.at[k], s, o).wait_recv()

    when_low(functools.partial(rim_land, 0))
    when_high(functools.partial(rim_land, 1))
    when_low(functools.partial(rim_land_on, 0))
    when_high(functools.partial(rim_land_on, 1))

    def act_copy(c):
        return remote(act.at[c], actp.at[c], a_s.at[c], a_r.at[c], pair, t)

    def hidden_tile(j):
        at = cols(j)
        first = dot_nn(rim[0, 0], w[0, pl.ds(0, H), at]) + dot_nn(rim[0, 1], w[0, pl.ds(H, H), at])
        last = dot_nn(rim[1, 0], w[2, pl.ds(0, H), at]) + dot_nn(rim[1, 1], w[2, pl.ds(H, H), at])
        hid[pl.ds(0, R), at] += first
        hid[pl.ds(T - R, R), at] += last
        value, derivative = gelu_pair(hid[:, at])
        value = value.astype(bf16)
        for i in range(per):
            act[per * j + i] = value[:, i * wide:(i + 1) * wide]
            act_copy(per * j + i).start()
        slope[:, at] = derivative

    hidden_tile(0)
    pl.when(t != early)(each(cot_pair, "start"))

    @pl.loop(1, tiles)
    def _(j):
        hidden_tile(j)

    remote(d.at[t], d.at[o], d_s, d_r, s, o).wait_recv()
    p_load.wait()

    @pl.loop(0, tiles)
    def _(j):
        grad = dot_nn(d[0], p[pl.ds(0, H), cols(j)]) + dot_nn(d[1], p[pl.ds(H, H), cols(j)])
        ghpad[pl.ds(R, T), cols(j)] = (grad * slope[:, cols(j)]).astype(bf16)

    gh_low = remote(
        ghpad.at[pl.ds(R, R), :], ghpad.at[pl.ds(R + T, R), :], gh_s.at[0], gh_r.at[1], s - 1, t
    )
    gh_high = remote(
        ghpad.at[pl.ds(T, R), :], ghpad.at[pl.ds(0, R), :], gh_s.at[1], gh_r.at[0], s + 1, t
    )
    when_low(gh_low.start)
    when_high(gh_high.start)

    def act_tile(i):
        return jnp.concatenate([act[per * i + k] for k in range(per)], axis=1)

    def mixed(at):
        total = dot_nt(act_tile(0), p[at, pl.ds(0, tile)])
        for i in range(1, tiles):
            total += dot_nt(act_tile(i), p[at, pl.ds(i * tile, tile)])
        return total.astype(bf16)

    def back(at):
        total = dot_nt(ghpad[pl.ds(2 * R, T), :], w[0, at, :])
        total += dot_nt(ghpad[pl.ds(R, T), :], w[1, at, :])
        total += dot_nt(ghpad[pl.ds(0, T), :], w[2, at, :])
        return total.astype(bf16)

    def rows_at(half, j):
        return pl.ds(pl.multiple_of(half * H + j * tile, tile), tile)

    m_side = remote(msend, mrecv, m_s, m_r, s, o)
    b_side = remote(bsend, brecv, b_s, b_r, s, o)

    def mixed_other():
        @pl.loop(0, tiles)
        def _(j):
            msend[:, cols(j)] = mixed(rows_at(o, j))
        m_side.start()

    def mixed_own():
        m_side.wait_recv()

        @pl.loop(0, tiles)
        def _(j):
            total = xpad[t, body, cols(j)].astype(f32) + mixed(rows_at(t, j)).astype(f32)
            out_ref[:, cols(j)] = (total + mrecv[:, cols(j)].astype(f32)).astype(bf16)

    def back_other(first, last):
        @pl.loop(first, last)
        def _(j):
            bsend[:, cols(j)] = back(rows_at(o, j))

    def back_own(first, last):
        @pl.loop(first, last)
        def _(j):
            total = d[t, :, cols(j)].astype(f32) + back(rows_at(t, j)).astype(f32)
            gi_ref[:, cols(j)] = (total + brecv[:, cols(j)].astype(f32)).astype(bf16)

    def gh_land():
        def land(k):
            remote(
                ghpad.at[pl.ds(R, R), :], ghpad.at[pl.ds(k * (R + T), R), :],
                gh_s.at[0], gh_r.at[k], s, o,
            ).wait_recv()
        when_low(functools.partial(land, 0))
        when_high(functools.partial(land, 1))

    def cot_land():
        def run():
            for i in range(2):
                cot_pair[i].wait_recv()
                cot_on[i].start()
        return run

    def cot_land_on():
        def run():
            for i in range(2):
                remote(
                    ct.at[2 * t + i, 1], ct.at[2 * o + i, 1], cf_s.at[i], cf_r.at[i], s, o
                ).wait_recv()
        return run

    def block(zd, c):
        return dot_nn(ct[zd, 0], act[c]) + dot_nn(ct[zd, 1], actp[c])

    def to_a(k, c, zt):
        return remote(gps.at[k, c], gpa.at[k, c], z_s.at[k, c], za_r.at[k, c], 2 * zt + y, t)

    def to_end(c, zt):
        return remote(gps.at[2, c], gpa.at[0, c], z_s.at[2, c], za_r.at[0, c], 2 * zt + y, t)

    def to_b(k, c, zt):
        return remote(gps.at[k, c], gpb.at[k, c], z_s.at[k, c], zb_r.at[k, c], 2 * zt + y, t)

    def head(c):
        @pl.when(outer)
        def _():
            act_copy(c).wait_recv()
            for k, zd in ((0, far_outer), (1, far_inner)):
                gps[k, c] = block(zd, c).astype(bf16)
                to_a(k, c, near_inner).start()

    def middle(c):
        @pl.when(inner)
        def _():
            act_copy(c).wait_recv()
            for k, zd in ((0, far_outer), (1, far_inner)):
                part = block(zd, c)
                to_a(k, c, near_inner).wait_recv()
                gps[k, c] = (part + gpa[k, c].astype(f32)).astype(bf16)
                to_b(k, c, far_inner).start()

    def near(c):
        gps[2, c] = block(near_inner, c).astype(bf16)
        to_a(2, c, near_inner).start()

    def back_to_end(c):
        part = block(near_outer, c)
        to_b(0, c, far_inner).wait_recv()
        gps[2, c] = (part + gpb[0, c].astype(f32)).astype(bf16)
        to_end(c, near_outer).start()

    def chunk_cols(c):
        return pl.ds(pl.multiple_of(c * wide, wide), wide)

    def own_block(c):
        gp_ref[:, chunk_cols(c)] = block(z, c)

    pl.when(t == early)(cot_land())
    mixed_other()
    pl.when(t != early)(cot_land_on())
    for i in range(2):
        remote(ct.at[2 * t + i, 0], ct.at[2 * o + i, 0], co_s.at[i], co_r.at[i], s, o).wait_recv()
    head(0)
    gh_land()
    back_other(0, 1)
    head(1)
    back_other(1, 2)
    head(2)
    back_other(2, 3)
    b_side.start()
    pl.when(t != early)(cot_land())
    head(3)
    mixed_own()
    middle(0)
    head(4)
    middle(1)
    back_own_ready = b_side.wait_recv
    back_own_ready()
    back_own(0, 1)
    head(5)
    pl.when(t == early)(cot_land_on())

    @pl.when(outer)
    def _():
        for c in range(chunks):
            near(c)

    middle(2)
    back_own(1, 2)
    middle(3)

    @pl.when(inner)
    def _():
        back_to_end(0)
        back_to_end(1)

    back_own(2, 3)
    middle(4)

    @pl.when(inner)
    def _():
        back_to_end(2)

    middle(5)

    @pl.when(inner)
    def _():
        for c in range(3, chunks):
            back_to_end(c)

    for c in range(chunks):
        own_block(c)

    for c in range(chunks):
        @pl.when(outer)
        def _():
            to_end(c, near_outer).wait_recv()
            gp_ref[:, chunk_cols(c)] += gpa[0, c].astype(f32)

        @pl.when(inner)
        def _():
            to_b(1, c, far_inner).wait_recv()
            part = gp_ref[:, chunk_cols(c)] + gpb[1, c].astype(f32)
            to_a(2, c, near_inner).wait_recv()
            gp_ref[:, chunk_cols(c)] = part + gpa[2, c].astype(f32)

    when_low(to_low.wait_send)
    when_high(to_high.wait_send)
    when_low(rim_on(0).wait_send)
    when_high(rim_on(1).wait_send)
    when_low(gh_low.wait_send)
    when_high(gh_high.wait_send)
    for copy in [x_side, d_side, m_side, b_side] + cot_pair + cot_on + cot_own:
        copy.wait_send()
    for c in range(chunks):
        act_copy(c).wait_send()
        for k in range(3):
            to_a(k, c, near_inner).wait_send()


def writer(out_ref, gi_ref, gp_ref, out_hbm, gi_hbm, gp_hbm, sem):
    copies = [
        pltpu.make_async_copy(src, dst, sem.at[i])
        for i, (src, dst) in enumerate(
            ((gp_ref, gp_hbm), (out_ref, out_hbm), (gi_ref, gi_hbm))
        )
    ]
    for copy in copies:
        copy.start()
    for copy in copies:
        copy.wait()


def local8(inputs, w_dilated, w_point, cotangent):
    T, H = inputs.shape
    C = w_point.shape[0]
    R = DILATION_BINS
    tile, wide = 256, 128
    tiles, chunks = H // tile, H // wide
    rows = C // 8
    bf16, f32 = jnp.bfloat16, jnp.float32
    dma = pltpu.SemaphoreType.DMA
    vmem = pl.BlockSpec(memory_space=pltpu.VMEM)
    hbm = pl.BlockSpec(memory_space=pltpu.HBM)
    shapes = [
        ((3, C, H), bf16), ((C, H), bf16), ((2, T + 2 * R, H), bf16), ((2, 2, R, H), bf16),
        ((T, H), f32), ((T, H), f32), ((chunks, T, wide), bf16), ((chunks, T, wide), bf16),
        ((2, T, H), bf16), ((H, T), bf16), ((4, 2, rows, T), bf16), ((T + 2 * R, H), bf16),
        ((T, H), bf16), ((T, H), bf16), ((T, H), bf16), ((T, H), bf16),
        ((3, chunks, rows, wide), bf16), ((3, chunks, rows, wide), bf16),
        ((2, chunks, rows, wide), bf16),
    ]
    one = dma(())
    two = dma((2,))
    sems = [
        dma((9,)), one, one, one, one, two, two, two, two, two, two,
        two, two, two, two, dma((chunks,)), dma((chunks,)), two, two, one, one, one, one,
        dma((3, chunks)), dma((3, chunks)), dma((2, chunks)),
    ]
    outs = [
        jax.ShapeDtypeStruct((T, H), bf16),
        jax.ShapeDtypeStruct((T, H), bf16),
        jax.ShapeDtypeStruct((rows, H), f32),
    ]
    results = pl.pallas_call(
        functools.partial(kernel8, tile),
        out_shape=[pltpu.VMEM(out.shape, out.dtype) for out in outs],
        in_specs=[hbm] * 4,
        out_specs=[vmem] * 3,
        scratch_shapes=[pltpu.VMEM(*shape) for shape in shapes] + sems,
        compiler_params=pltpu.CompilerParams(
            collective_id=0, has_side_effects=True, vmem_limit_bytes=60 * 1024 * 1024
        ),
    )(inputs, jnp.transpose(w_dilated, (1, 0, 2)), w_point, cotangent)
    return tuple(
        pl.pallas_call(
            writer,
            out_shape=outs,
            in_specs=[vmem] * 3,
            out_specs=[hbm] * 3,
            scratch_shapes=[dma((3,))],
            compiler_params=pltpu.CompilerParams(vmem_limit_bytes=1024 * 1024),
        )(*results)
    )


def local(n, inputs, w_dilated, w_point, cotangent):
    if n == 8 and inputs.shape[0] == 256:
        return local8(inputs, w_dilated, w_point, cotangent)
    T, H = inputs.shape
    C = w_point.shape[0]
    R = DILATION_BINS
    tile = 256
    tiles = H // tile
    rows = C // n
    bf16, f32 = jnp.bfloat16, jnp.float32
    with_point = rows % 16 == 0 and n % 2 == 0
    nz = n // 2
    vmem = pl.BlockSpec(memory_space=pltpu.VMEM)
    hbm = pl.BlockSpec(memory_space=pl.ANY)
    plane = jax.ShapeDtypeStruct((T, H), bf16)
    act_shape = (tiles, T, tile)
    outs = [plane, plane]
    scratch = []
    if with_point:
        outs += [jax.ShapeDtypeStruct((rows, H), f32)]
        scratch += [pltpu.VMEM(act_shape, bf16), pltpu.VMEM((T, C), bf16)]
    else:
        outs += [jax.ShapeDtypeStruct(act_shape, bf16), jax.ShapeDtypeStruct((T, C), bf16)]
    dma = pltpu.SemaphoreType.DMA
    scratch += [
        pltpu.VMEM((3, C, H), bf16),
        pltpu.VMEM((C, H), bf16),
        pltpu.VMEM((T + 2 * R, C), bf16),
        pltpu.VMEM((T, H), f32),
        pltpu.VMEM((T + 2 * R, H), bf16),
        pltpu.VMEM((T, H), bf16),
        pltpu.VMEM((T, H), bf16),
        pltpu.VMEM((T, H), bf16),
        pltpu.VMEM((T, H), bf16),
        dma((4,)), dma((6,)), dma((6,)), dma((4,)), dma((4,)), dma((2,)), dma((2,)),
    ]
    if with_point:
        scratch += [
            pltpu.VMEM(act_shape, bf16),
            pltpu.VMEM((T, H), bf16),
            pltpu.VMEM((T, H), bf16),
            pltpu.VMEM((C, 2 * T), bf16),
            pltpu.VMEM((nz - 1, tiles, rows, tile), bf16),
            pltpu.VMEM((nz - 1, tiles, rows, tile), bf16),
            dma((tiles,)), dma((tiles,)), dma((nz - 1, tiles)), dma((nz - 1, tiles)),
        ]
    results = pl.pallas_call(
        functools.partial(kernel, n, tile, with_point),
        out_shape=outs,
        in_specs=[vmem, hbm, hbm, vmem],
        out_specs=[vmem] * len(outs),
        scratch_shapes=scratch,
        compiler_params=pltpu.CompilerParams(
            collective_id=0, has_side_effects=True, vmem_limit_bytes=48 * 1024 * 1024
        ),
    )(inputs, jnp.transpose(w_dilated, (1, 0, 2)), w_point, cotangent)
    if with_point:
        return tuple(results)
    output, grad_inputs, act, full_grad = results
    activation = jnp.transpose(act, (1, 0, 2)).reshape(T, H)
    grad_point = lax.psum_scatter(
        jnp.einsum("to,tc->oc", full_grad, activation, preferred_element_type=f32),
        "seq",
        scatter_dimension=0,
        tiled=True,
    )
    return (output, grad_inputs, grad_point)


def solution(mesh):
    placed = (
        P(("groups", "seq"), "tensor"),
        P(None, None, "tensor"),
        P(None, "tensor"),
        P(("groups", "seq"), "tensor"),
    )
    return jax.shard_map(
        functools.partial(local, mesh.shape["seq"]),
        mesh=mesh,
        in_specs=placed,
        out_specs=(
            P(("groups", "seq"), "tensor"),
            P(("groups", "seq"), "tensor"),
            P(("groups", "seq"), "tensor"),
        ),
        check_vma=False,
    )
```

```python
import functools
import math

import jax
import jax.numpy as jnp
from jax import lax
from jax.experimental import pallas as pl
from jax.experimental.pallas import tpu as pltpu
from jax.sharding import PartitionSpec as P

DILATION_BINS = 32
MESH = pl.DeviceIdType.MESH

gelu_cubic = 0.044715
gelu_scale = math.sqrt(2.0 / math.pi)


def gelu_pair(values):
    square = values * values
    tangent = jnp.tanh(gelu_scale * (values + gelu_cubic * square * values))
    half = 0.5 * (1.0 + tangent)
    slope = half + 0.5 * values * (1.0 - tangent * tangent) * gelu_scale * (
        1.0 + 3.0 * gelu_cubic * square
    )
    return values * half, slope


def dot_nn(a, b):
    return jnp.dot(a, b, preferred_element_type=jnp.float32)


def dot_nt(a, b):
    return lax.dot_general(a, b, (((1,), (1,)), ((), ())), preferred_element_type=jnp.float32)


def kernel(n, tile, with_point, *refs):
    x_ref, w_hbm, p_hbm, d_ref = refs[:4]
    if with_point:
        out_ref, gi_ref, gp_ref = refs[4:7]
        act, dfull = refs[7:9]
        rest = refs[9:]
    else:
        out_ref, gi_ref, act, dfull = refs[4:8]
        rest = refs[8:]
    (w, p, xfull, slope, ghpad, msend, mrecv, bsend, brecv) = rest[:9]
    (lsem, ssem, rsem, xs_sem, xr_sem, gs_sem, gr_sem) = rest[9:16]
    if with_point:
        (actp, dp, dps, cot_t, gps, gpr, as_sem, ar_sem, ps_sem, pr_sem) = rest[16:]

    s = lax.axis_index("seq")
    t = lax.axis_index("tensor")
    o = 1 - t
    T, H = x_ref.shape
    C = 2 * H
    R = DILATION_BINS
    tiles = H // tile
    bf16 = jnp.bfloat16
    has_low = s > 0
    has_high = s < n - 1
    mine = pl.ds(pl.multiple_of(t * H, H), H)
    other = pl.ds(pl.multiple_of(o * H, H), H)
    nz = n // 2
    z = s // 2
    y = lax.rem(s, 2)
    pair = s + 1 - 2 * y

    def remote(src, dst, send, recv, seq, tensor):
        return pltpu.make_async_remote_copy(
            src_ref=src,
            dst_ref=dst,
            send_sem=send,
            recv_sem=recv,
            device_id={"seq": seq, "tensor": tensor},
            device_id_type=MESH,
        )

    def cols(j):
        return pl.ds(pl.multiple_of(j * tile, tile), tile)

    w_loads = [pltpu.make_async_copy(w_hbm.at[k], w.at[k], lsem.at[k]) for k in range(3)]
    p_load = pltpu.make_async_copy(p_hbm, p, lsem.at[3])
    for load in w_loads:
        load.start()
    p_load.start()

    barrier = pltpu.get_barrier_semaphore()

    def greet(seq, tensor):
        pl.semaphore_signal(
            barrier, inc=1, device_id={"seq": seq, "tensor": tensor}, device_id_type=MESH
        )

    greet(s, o)

    @pl.when(has_low)
    def _():
        greet(s - 1, t)
        greet(s - 1, o)

    @pl.when(has_high)
    def _():
        greet(s + 1, t)
        greet(s + 1, o)

    if with_point:
        for d in range(1, nz):
            greet(lax.rem(z + d, nz) * 2 + y, t)
    xfull[pl.ds(R, T), mine] = x_ref[...]
    dfull[:, mine] = d_ref[...]
    sides = lax.div(s + n - 1, n) + lax.div(2 * n - 2 - s, n)
    pl.semaphore_wait(barrier, 1 + (nz - 1 if with_point else 0) + 2 * sides)

    def to_low(slot, tensor):
        return remote(
            x_ref.at[pl.ds(0, R), :], xfull.at[pl.ds(R + T, R), mine],
            xs_sem.at[slot], xr_sem.at[2 + t], s - 1, tensor,
        )

    def to_high(slot, tensor):
        return remote(
            x_ref.at[pl.ds(T - R, R), :], xfull.at[pl.ds(0, R), mine],
            xs_sem.at[2 + slot], xr_sem.at[t], s + 1, tensor,
        )

    @pl.when(has_low)
    def _():
        to_low(0, t).start()
        to_low(1, o).start()

    @pl.when(has_high)
    def _():
        to_high(0, t).start()
        to_high(1, o).start()

    x_side = remote(x_ref, xfull.at[pl.ds(R, T), mine], ssem.at[0], rsem.at[0], s, o)
    x_side.start()
    d_side = remote(d_ref, dfull.at[:, mine], ssem.at[1], rsem.at[1], s, o)
    d_side.start()
    if with_point:
        d_pair = remote(d_ref, dp, ssem.at[2], rsem.at[2], pair, t)
        d_pair.start()
        d_next = remote(dp, dps, ssem.at[3], rsem.at[3], s, o)
        cot_t[mine, pl.ds(0, T)] = d_ref[...].T

    @pl.when(s == 0)
    def _():
        xfull[pl.ds(0, R), :] = jnp.zeros((R, C), bf16)
        ghpad[pl.ds(0, R), :] = jnp.zeros((R, H), bf16)

    @pl.when(s == n - 1)
    def _():
        xfull[pl.ds(R + T, R), :] = jnp.zeros((R, C), bf16)
        ghpad[pl.ds(R + T, R), :] = jnp.zeros((R, H), bf16)

    remote(x_ref, xfull.at[pl.ds(R, T), other], ssem.at[0], rsem.at[0], s, o).wait_recv()

    @pl.when(has_low)
    def _():
        for half in range(2):
            remote(
                x_ref.at[pl.ds(0, R), :], xfull.at[pl.ds(0, R), pl.ds(half * H, H)],
                xs_sem.at[0], xr_sem.at[half], s - 1, t,
            ).wait_recv()

    @pl.when(has_high)
    def _():
        for half in range(2):
            remote(
                x_ref.at[pl.ds(0, R), :], xfull.at[pl.ds(R + T, R), pl.ds(half * H, H)],
                xs_sem.at[0], xr_sem.at[2 + half], s + 1, t,
            ).wait_recv()

    for load in w_loads:
        load.wait()

    def act_copy(j):
        return remote(
            act.at[j], actp.at[j], as_sem.at[j], ar_sem.at[j], pair, t
        )

    @pl.loop(0, tiles)
    def _(j):
        hidden = dot_nn(xfull[pl.ds(0, T), :], w[0, :, cols(j)])
        hidden += dot_nn(xfull[pl.ds(R, T), :], w[1, :, cols(j)])
        hidden += dot_nn(xfull[pl.ds(2 * R, T), :], w[2, :, cols(j)])
        value, derivative = gelu_pair(hidden)
        act[j] = value.astype(bf16)
        slope[:, cols(j)] = derivative
        if with_point:
            act_copy(j).start()

    if with_point:
        remote(d_ref, dp, ssem.at[2], rsem.at[2], pair, t).wait_recv()
        d_next.start()
        cot_t[mine, pl.ds(T, T)] = dp[...].T
    remote(d_ref, dfull.at[:, other], ssem.at[1], rsem.at[1], s, o).wait_recv()
    p_load.wait()
    if with_point:
        cot_t[other, pl.ds(0, T)] = dfull[:, other].T

    @pl.loop(0, tiles)
    def _(j):
        grad = dot_nn(dfull[...], p[:, cols(j)]) * slope[:, cols(j)]
        ghpad[pl.ds(R, T), cols(j)] = grad.astype(bf16)

    gh_low = remote(
        ghpad.at[pl.ds(R, R), :], ghpad.at[pl.ds(R + T, R), :],
        gs_sem.at[0], gr_sem.at[1], s - 1, t,
    )
    gh_high = remote(
        ghpad.at[pl.ds(T, R), :], ghpad.at[pl.ds(0, R), :],
        gs_sem.at[1], gr_sem.at[0], s + 1, t,
    )

    @pl.when(has_low)
    def _():
        gh_low.start()

    @pl.when(has_high)
    def _():
        gh_high.start()

    def point_copy(d, j):
        return remote(
            gps.at[d - 1, j], gpr.at[d - 1, j], ps_sem.at[d - 1, j], pr_sem.at[d - 1, j],
            lax.rem(z + d, nz) * 2 + y, t,
        )

    if with_point:
        rows = gp_ref.shape[0]
        remote(dp, dps, ssem.at[3], rsem.at[3], s, o).wait_recv()
        cot_t[other, pl.ds(T, T)] = dps[...].T

        @pl.loop(0, tiles)
        def _(j):
            act_copy(j).wait_recv()

            def block(d):
                owner = lax.rem(z + d, nz) * 2 + y
                at = pl.ds(pl.multiple_of(owner * rows, rows), rows)
                return dot_nn(cot_t[at, pl.ds(0, T)], act[j]) + dot_nn(
                    cot_t[at, pl.ds(T, T)], actp[j]
                )

            for d in range(1, nz):
                gps[d - 1, j] = block(d).astype(bf16)
                point_copy(d, j).start()
            gp_ref[:, cols(j)] = block(0)

    def mixed(at):
        total = dot_nt(act[0], p[at, pl.ds(0, tile)])
        for i in range(1, tiles):
            total += dot_nt(act[i], p[at, pl.ds(i * tile, tile)])
        return total.astype(bf16)

    @pl.loop(0, tiles)
    def _(j):
        msend[:, cols(j)] = mixed(pl.ds(pl.multiple_of(o * H + j * tile, tile), tile))

    m_side = remote(msend, mrecv, ssem.at[4], rsem.at[4], s, o)
    m_side.start()

    @pl.when(has_low)
    def _():
        remote(
            ghpad.at[pl.ds(R, R), :], ghpad.at[pl.ds(0, R), :],
            gs_sem.at[0], gr_sem.at[0], s - 1, t,
        ).wait_recv()

    @pl.when(has_high)
    def _():
        remote(
            ghpad.at[pl.ds(R, R), :], ghpad.at[pl.ds(R + T, R), :],
            gs_sem.at[0], gr_sem.at[1], s + 1, t,
        ).wait_recv()

    def back(at):
        total = dot_nt(ghpad[pl.ds(2 * R, T), :], w[0, at, :])
        total += dot_nt(ghpad[pl.ds(R, T), :], w[1, at, :])
        total += dot_nt(ghpad[pl.ds(0, T), :], w[2, at, :])
        return total.astype(bf16)

    @pl.loop(0, tiles)
    def _(j):
        bsend[:, cols(j)] = back(pl.ds(pl.multiple_of(o * H + j * tile, tile), tile))

    b_side = remote(bsend, brecv, ssem.at[5], rsem.at[5], s, o)
    b_side.start()
    m_side.wait_recv()

    @pl.loop(0, tiles)
    def _(j):
        own = mixed(pl.ds(pl.multiple_of(t * H + j * tile, tile), tile))
        total = x_ref[:, cols(j)].astype(jnp.float32) + own.astype(jnp.float32)
        out_ref[:, cols(j)] = (total + mrecv[:, cols(j)].astype(jnp.float32)).astype(bf16)

    b_side.wait_recv()

    @pl.loop(0, tiles)
    def _(j):
        own = back(pl.ds(pl.multiple_of(t * H + j * tile, tile), tile))
        total = d_ref[:, cols(j)].astype(jnp.float32) + own.astype(jnp.float32)
        gi_ref[:, cols(j)] = (total + brecv[:, cols(j)].astype(jnp.float32)).astype(bf16)

    if with_point:

        @pl.loop(0, tiles)
        def _(j):
            total = gp_ref[:, cols(j)]
            for d in range(1, nz):
                point_copy(d, j).wait_recv()
                total += gpr[d - 1, j].astype(jnp.float32)
            gp_ref[:, cols(j)] = total

    @pl.when(has_low)
    def _():
        to_low(0, t).wait_send()
        to_low(1, o).wait_send()
        gh_low.wait_send()

    @pl.when(has_high)
    def _():
        to_high(0, t).wait_send()
        to_high(1, o).wait_send()
        gh_high.wait_send()

    x_side.wait_send()
    d_side.wait_send()
    m_side.wait_send()
    b_side.wait_send()
    if with_point:
        d_pair.wait_send()
        d_next.wait_send()

        @pl.loop(0, tiles)
        def _(j):
            act_copy(j).wait_send()
            for d in range(1, nz):
                point_copy(d, j).wait_send()


def kernel8(tile, *refs):
    x_hbm, w_hbm, p_hbm, d_hbm, out_ref, gi_ref, gp_ref = refs[:7]
    (w, p, xpad, rim, hid, slope, act, actp, d, dt, ct, ghpad) = refs[7:19]
    (msend, mrecv, bsend, brecv, gps, gpa, gpb) = refs[19:26]
    (load, x_s, x_r, d_s, d_r, rim_s, rim_r, rimf_s, rimf_r, co_s, co_r) = refs[26:37]
    (cp_s, cp_r, cf_s, cf_r, a_s, a_r, gh_s, gh_r, m_s, m_r, b_s, b_r) = refs[37:49]
    (z_s, za_r, zb_r) = refs[49:]

    s = lax.axis_index("seq")
    t = lax.axis_index("tensor")
    o = 1 - t
    z = s // 2
    y = lax.rem(s, 2)
    pair = s + 1 - 2 * y
    T, H = out_ref.shape
    R = DILATION_BINS
    rows = gp_ref.shape[0]
    tiles = H // tile
    chunks, wide = act.shape[0], act.shape[2]
    per = tile // wide
    bf16, f32 = jnp.bfloat16, jnp.float32
    low = s > 0
    high = s < 7
    outer = lax.rem(z + 1, 4) < 2
    inner = lax.rem(z + 1, 4) >= 2
    upper = z // 2
    far_outer = 3 - 3 * upper
    far_inner = 2 - upper
    near_inner = 1 + upper
    near_outer = 3 * upper
    early = 1 - upper

    def remote(src, dst, send, recv, seq, tensor):
        return pltpu.make_async_remote_copy(
            src_ref=src, dst_ref=dst, send_sem=send, recv_sem=recv,
            device_id={"seq": seq, "tensor": tensor}, device_id_type=MESH,
        )

    def cols(j):
        return pl.ds(pl.multiple_of(j * tile, tile), tile)

    barrier = pltpu.get_barrier_semaphore()

    def greet(seq, tensor):
        pl.semaphore_signal(
            barrier, inc=1, device_id={"seq": seq, "tensor": tensor}, device_id_type=MESH
        )

    greet(pair, t)

    @pl.when(z > 0)
    def _():
        greet(s - 2, t)

    @pl.when(z < 3)
    def _():
        greet(s + 2, t)

    @pl.when(jnp.logical_and(y == 0, z > 0))
    def _():
        greet(s - 1, t)

    @pl.when(jnp.logical_and(y == 1, z < 3))
    def _():
        greet(s + 1, t)

    greet(s, o)

    own = pl.ds(pl.multiple_of(t * H, H), H)
    other = pl.ds(pl.multiple_of(o * H, H), H)
    body = pl.ds(R, T)
    x_load = pltpu.make_async_copy(x_hbm, xpad.at[t, body], load.at[0])
    d_load = pltpu.make_async_copy(d_hbm, d.at[t], load.at[1])
    w_own = [
        pltpu.make_async_copy(w_hbm.at[k, own], w.at[k, own], load.at[2 + k]) for k in range(3)
    ]
    w_other = [
        pltpu.make_async_copy(w_hbm.at[k, other], w.at[k, other], load.at[5 + k])
        for k in range(3)
    ]
    p_load = pltpu.make_async_copy(p_hbm, p, load.at[8])
    for copy in [d_load, x_load] + w_own + w_other + [p_load]:
        copy.start()

    for half in range(2):
        xpad[half, pl.ds(0, R)] = jnp.zeros((R, H), bf16)
        xpad[half, pl.ds(R + T, R)] = jnp.zeros((R, H), bf16)

    @pl.when(s == 0)
    def _():
        rim[0] = jnp.zeros((2, R, H), bf16)
        ghpad[pl.ds(0, R), :] = jnp.zeros((R, H), bf16)

    @pl.when(s == 7)
    def _():
        rim[1] = jnp.zeros((2, R, H), bf16)
        ghpad[pl.ds(R + T, R), :] = jnp.zeros((R, H), bf16)

    d_load.wait()
    dt[...] = d[t].T

    def dt_block(i, side):
        return pl.ds(pl.multiple_of((2 * i + side) * rows, rows), rows)

    for i in range(2):
        ct[2 * t + i, 0] = dt[dt_block(i, y), :]

    x_load.wait()
    for copy in w_own:
        copy.wait()

    def taps(half, rows_of, j):
        total = dot_nn(xpad[half, pl.ds(0, T)], w[0, rows_of, cols(j)])
        total += dot_nn(xpad[half, pl.ds(R, T)], w[1, rows_of, cols(j)])
        return total + dot_nn(xpad[half, pl.ds(2 * R, T)], w[2, rows_of, cols(j)])

    @pl.loop(0, tiles)
    def _(j):
        hid[:, cols(j)] = taps(t, own, j)

    met = 2 + jnp.where(z > 0, 1, 0) + jnp.where(z < 3, 1, 0)
    pl.semaphore_wait(barrier, met + jnp.where(jnp.where(y == 0, z > 0, z < 3), 1, 0))

    to_low = remote(
        xpad.at[t, pl.ds(R, R)], rim.at[1, t], rim_s.at[0], rim_r.at[1], s - 1, t
    )
    to_high = remote(
        xpad.at[t, pl.ds(T, R)], rim.at[0, t], rim_s.at[1], rim_r.at[0], s + 1, t
    )

    def when_low(act_on):
        pl.when(low)(act_on)

    def when_high(act_on):
        pl.when(high)(act_on)

    when_low(to_low.start)
    when_high(to_high.start)
    x_side = remote(xpad.at[t, body], xpad.at[t, body], x_s, x_r, s, o)
    x_side.start()

    cot_pair = [
        remote(dt.at[dt_block(i, 1 - y), :], ct.at[2 * t + i, 1], cp_s.at[i], cp_r.at[i], pair, t)
        for i in range(2)
    ]
    cot_on = [
        remote(ct.at[2 * t + i, 1], ct.at[2 * t + i, 1], cf_s.at[i], cf_r.at[i], s, o)
        for i in range(2)
    ]
    cot_own = [
        remote(ct.at[2 * t + i, 0], ct.at[2 * t + i, 0], co_s.at[i], co_r.at[i], s, o)
        for i in range(2)
    ]

    def each(copies, what):
        def run():
            for copy in copies:
                getattr(copy, what)()
        return run

    pl.when(t == early)(each(cot_pair, "start"))
    d_side = remote(d.at[t], d.at[t], d_s, d_r, s, o)
    d_side.start()
    each(cot_own, "start")()

    remote(xpad.at[t, body], xpad.at[o, body], x_s, x_r, s, o).wait_recv()
    for copy in w_other:
        copy.wait()

    @pl.loop(0, tiles)
    def _(j):
        hid[:, cols(j)] += taps(o, other, j)

    def rim_on(k):
        return remote(rim.at[k, t], rim.at[k, t], rimf_s.at[k], rimf_r.at[k], s, o)

    def rim_land(k):
        remote(xpad.at[t, pl.ds(R, R)], rim.at[k, t], rim_s.at[0], rim_r.at[k], s, o).wait_recv()
        rim_on(k).start()

    def rim_land_on(k):
        remote(rim.at[k, t], rim.at[k, o], rimf_s.at[k], rimf_r.at[k], s, o).wait_recv()

    when_low(functools.partial(rim_land, 0))
    when_high(functools.partial(rim_land, 1))
    when_low(functools.partial(rim_land_on, 0))
    when_high(functools.partial(rim_land_on, 1))

    def act_copy(c):
        return remote(act.at[c], actp.at[c], a_s.at[c], a_r.at[c], pair, t)

    def hidden_tile(j):
        at = cols(j)
        first = dot_nn(rim[0, 0], w[0, pl.ds(0, H), at]) + dot_nn(rim[0, 1], w[0, pl.ds(H, H), at])
        last = dot_nn(rim[1, 0], w[2, pl.ds(0, H), at]) + dot_nn(rim[1, 1], w[2, pl.ds(H, H), at])
        hid[pl.ds(0, R), at] += first
        hid[pl.ds(T - R, R), at] += last
        value, derivative = gelu_pair(hid[:, at])
        value = value.astype(bf16)
        for i in range(per):
            act[per * j + i] = value[:, i * wide:(i + 1) * wide]
            act_copy(per * j + i).start()
        slope[:, at] = derivative

    hidden_tile(0)
    pl.when(t != early)(each(cot_pair, "start"))

    @pl.loop(1, tiles)
    def _(j):
        hidden_tile(j)

    remote(d.at[t], d.at[o], d_s, d_r, s, o).wait_recv()
    p_load.wait()

    @pl.loop(0, tiles)
    def _(j):
        grad = dot_nn(d[0], p[pl.ds(0, H), cols(j)]) + dot_nn(d[1], p[pl.ds(H, H), cols(j)])
        ghpad[pl.ds(R, T), cols(j)] = (grad * slope[:, cols(j)]).astype(bf16)

    gh_low = remote(
        ghpad.at[pl.ds(R, R), :], ghpad.at[pl.ds(R + T, R), :], gh_s.at[0], gh_r.at[1], s - 1, t
    )
    gh_high = remote(
        ghpad.at[pl.ds(T, R), :], ghpad.at[pl.ds(0, R), :], gh_s.at[1], gh_r.at[0], s + 1, t
    )
    when_low(gh_low.start)
    when_high(gh_high.start)

    def act_tile(i):
        return jnp.concatenate([act[per * i + k] for k in range(per)], axis=1)

    def mixed(at):
        total = dot_nt(act_tile(0), p[at, pl.ds(0, tile)])
        for i in range(1, tiles):
            total += dot_nt(act_tile(i), p[at, pl.ds(i * tile, tile)])
        return total.astype(bf16)

    def back(at):
        total = dot_nt(ghpad[pl.ds(2 * R, T), :], w[0, at, :])
        total += dot_nt(ghpad[pl.ds(R, T), :], w[1, at, :])
        total += dot_nt(ghpad[pl.ds(0, T), :], w[2, at, :])
        return total.astype(bf16)

    def rows_at(half, j):
        return pl.ds(pl.multiple_of(half * H + j * tile, tile), tile)

    m_side = remote(msend, mrecv, m_s, m_r, s, o)
    b_side = remote(bsend, brecv, b_s, b_r, s, o)

    def mixed_other():
        @pl.loop(0, tiles)
        def _(j):
            msend[:, cols(j)] = mixed(rows_at(o, j))
        m_side.start()

    def mixed_own():
        m_side.wait_recv()

        @pl.loop(0, tiles)
        def _(j):
            total = xpad[t, body, cols(j)].astype(f32) + mixed(rows_at(t, j)).astype(f32)
            out_ref[:, cols(j)] = (total + mrecv[:, cols(j)].astype(f32)).astype(bf16)

    def back_other(first, last):
        @pl.loop(first, last)
        def _(j):
            bsend[:, cols(j)] = back(rows_at(o, j))

    def back_own(first, last):
        @pl.loop(first, last)
        def _(j):
            total = d[t, :, cols(j)].astype(f32) + back(rows_at(t, j)).astype(f32)
            gi_ref[:, cols(j)] = (total + brecv[:, cols(j)].astype(f32)).astype(bf16)

    def gh_land():
        def land(k):
            remote(
                ghpad.at[pl.ds(R, R), :], ghpad.at[pl.ds(k * (R + T), R), :],
                gh_s.at[0], gh_r.at[k], s, o,
            ).wait_recv()
        when_low(functools.partial(land, 0))
        when_high(functools.partial(land, 1))

    def cot_land():
        def run():
            for i in range(2):
                cot_pair[i].wait_recv()
                cot_on[i].start()
        return run

    def cot_land_on():
        def run():
            for i in range(2):
                remote(
                    ct.at[2 * t + i, 1], ct.at[2 * o + i, 1], cf_s.at[i], cf_r.at[i], s, o
                ).wait_recv()
        return run

    def block(zd, c):
        return dot_nn(ct[zd, 0], act[c]) + dot_nn(ct[zd, 1], actp[c])

    def to_a(k, c, zt):
        return remote(gps.at[k, c], gpa.at[k, c], z_s.at[k, c], za_r.at[k, c], 2 * zt + y, t)

    def to_end(c, zt):
        return remote(gps.at[2, c], gpa.at[0, c], z_s.at[2, c], za_r.at[0, c], 2 * zt + y, t)

    def to_b(k, c, zt):
        return remote(gps.at[k, c], gpb.at[k, c], z_s.at[k, c], zb_r.at[k, c], 2 * zt + y, t)

    def head(c):
        @pl.when(outer)
        def _():
            act_copy(c).wait_recv()
            for k, zd in ((0, far_outer), (1, far_inner)):
                gps[k, c] = block(zd, c).astype(bf16)
                to_a(k, c, near_inner).start()

    def middle(c):
        @pl.when(inner)
        def _():
            act_copy(c).wait_recv()
            for k, zd in ((0, far_outer), (1, far_inner)):
                part = block(zd, c)
                to_a(k, c, near_inner).wait_recv()
                gps[k, c] = (part + gpa[k, c].astype(f32)).astype(bf16)
                to_b(k, c, far_inner).start()

    def near(c):
        gps[2, c] = block(near_inner, c).astype(bf16)
        to_a(2, c, near_inner).start()

    def back_to_end(c):
        part = block(near_outer, c)
        to_b(0, c, far_inner).wait_recv()
        gps[2, c] = (part + gpb[0, c].astype(f32)).astype(bf16)
        to_end(c, near_outer).start()

    def chunk_cols(c):
        return pl.ds(pl.multiple_of(c * wide, wide), wide)

    def own_block(c):
        gp_ref[:, chunk_cols(c)] = block(z, c)

    pl.when(t == early)(cot_land())
    mixed_other()
    pl.when(t != early)(cot_land_on())
    for i in range(2):
        remote(ct.at[2 * t + i, 0], ct.at[2 * o + i, 0], co_s.at[i], co_r.at[i], s, o).wait_recv()
    head(0)
    head(1)
    mixed_own()
    pl.when(t != early)(cot_land())
    head(2)
    head(3)
    middle(0)
    head(4)
    middle(1)
    head(5)
    pl.when(t == early)(cot_land_on())

    @pl.when(outer)
    def _():
        for c in range(chunks):
            near(c)

    middle(2)
    gh_land()
    back_other(0, 1)
    middle(3)

    @pl.when(inner)
    def _():
        back_to_end(0)
        back_to_end(1)

    back_other(1, 3)
    b_side.start()
    middle(4)

    @pl.when(inner)
    def _():
        back_to_end(2)
        back_to_end(3)

    middle(5)
    b_side.wait_recv()
    back_own(0, 2)

    @pl.when(inner)
    def _():
        back_to_end(4)

    back_own(2, 3)

    @pl.when(inner)
    def _():
        back_to_end(5)

    for c in range(chunks):
        own_block(c)

    for c in range(chunks):
        @pl.when(outer)
        def _():
            to_end(c, near_outer).wait_recv()
            gp_ref[:, chunk_cols(c)] += gpa[0, c].astype(f32)

        @pl.when(inner)
        def _():
            to_b(1, c, far_inner).wait_recv()
            part = gp_ref[:, chunk_cols(c)] + gpb[1, c].astype(f32)
            to_a(2, c, near_inner).wait_recv()
            gp_ref[:, chunk_cols(c)] = part + gpa[2, c].astype(f32)

    when_low(to_low.wait_send)
    when_high(to_high.wait_send)
    when_low(rim_on(0).wait_send)
    when_high(rim_on(1).wait_send)
    when_low(gh_low.wait_send)
    when_high(gh_high.wait_send)
    for copy in [x_side, d_side, m_side, b_side] + cot_pair + cot_on + cot_own:
        copy.wait_send()
    for c in range(chunks):
        act_copy(c).wait_send()
        for k in range(3):
            to_a(k, c, near_inner).wait_send()


def writer(out_ref, gi_ref, gp_ref, out_hbm, gi_hbm, gp_hbm, sem):
    copies = [
        pltpu.make_async_copy(src, dst, sem.at[i])
        for i, (src, dst) in enumerate(
            ((gp_ref, gp_hbm), (out_ref, out_hbm), (gi_ref, gi_hbm))
        )
    ]
    for copy in copies:
        copy.start()
    for copy in copies:
        copy.wait()


def local8(inputs, w_dilated, w_point, cotangent):
    T, H = inputs.shape
    C = w_point.shape[0]
    R = DILATION_BINS
    tile, wide = 256, 128
    tiles, chunks = H // tile, H // wide
    rows = C // 8
    bf16, f32 = jnp.bfloat16, jnp.float32
    dma = pltpu.SemaphoreType.DMA
    vmem = pl.BlockSpec(memory_space=pltpu.VMEM)
    hbm = pl.BlockSpec(memory_space=pltpu.HBM)
    shapes = [
        ((3, C, H), bf16), ((C, H), bf16), ((2, T + 2 * R, H), bf16), ((2, 2, R, H), bf16),
        ((T, H), f32), ((T, H), f32), ((chunks, T, wide), bf16), ((chunks, T, wide), bf16),
        ((2, T, H), bf16), ((H, T), bf16), ((4, 2, rows, T), bf16), ((T + 2 * R, H), bf16),
        ((T, H), bf16), ((T, H), bf16), ((T, H), bf16), ((T, H), bf16),
        ((3, chunks, rows, wide), bf16), ((3, chunks, rows, wide), bf16),
        ((2, chunks, rows, wide), bf16),
    ]
    one = dma(())
    two = dma((2,))
    sems = [
        dma((9,)), one, one, one, one, two, two, two, two, two, two,
        two, two, two, two, dma((chunks,)), dma((chunks,)), two, two, one, one, one, one,
        dma((3, chunks)), dma((3, chunks)), dma((2, chunks)),
    ]
    outs = [
        jax.ShapeDtypeStruct((T, H), bf16),
        jax.ShapeDtypeStruct((T, H), bf16),
        jax.ShapeDtypeStruct((rows, H), f32),
    ]
    results = pl.pallas_call(
        functools.partial(kernel8, tile),
        out_shape=[pltpu.VMEM(out.shape, out.dtype) for out in outs],
        in_specs=[hbm] * 4,
        out_specs=[vmem] * 3,
        scratch_shapes=[pltpu.VMEM(*shape) for shape in shapes] + sems,
        compiler_params=pltpu.CompilerParams(
            collective_id=0, has_side_effects=True, vmem_limit_bytes=60 * 1024 * 1024
        ),
    )(inputs, jnp.transpose(w_dilated, (1, 0, 2)), w_point, cotangent)
    return tuple(
        pl.pallas_call(
            writer,
            out_shape=outs,
            in_specs=[vmem] * 3,
            out_specs=[hbm] * 3,
            scratch_shapes=[dma((3,))],
            compiler_params=pltpu.CompilerParams(vmem_limit_bytes=1024 * 1024),
        )(*results)
    )


def local(n, inputs, w_dilated, w_point, cotangent):
    if n == 8 and inputs.shape[0] == 256:
        return local8(inputs, w_dilated, w_point, cotangent)
    T, H = inputs.shape
    C = w_point.shape[0]
    R = DILATION_BINS
    tile = 256
    tiles = H // tile
    rows = C // n
    bf16, f32 = jnp.bfloat16, jnp.float32
    with_point = rows % 16 == 0 and n % 2 == 0
    nz = n // 2
    vmem = pl.BlockSpec(memory_space=pltpu.VMEM)
    hbm = pl.BlockSpec(memory_space=pl.ANY)
    plane = jax.ShapeDtypeStruct((T, H), bf16)
    act_shape = (tiles, T, tile)
    outs = [plane, plane]
    scratch = []
    if with_point:
        outs += [jax.ShapeDtypeStruct((rows, H), f32)]
        scratch += [pltpu.VMEM(act_shape, bf16), pltpu.VMEM((T, C), bf16)]
    else:
        outs += [jax.ShapeDtypeStruct(act_shape, bf16), jax.ShapeDtypeStruct((T, C), bf16)]
    dma = pltpu.SemaphoreType.DMA
    scratch += [
        pltpu.VMEM((3, C, H), bf16),
        pltpu.VMEM((C, H), bf16),
        pltpu.VMEM((T + 2 * R, C), bf16),
        pltpu.VMEM((T, H), f32),
        pltpu.VMEM((T + 2 * R, H), bf16),
        pltpu.VMEM((T, H), bf16),
        pltpu.VMEM((T, H), bf16),
        pltpu.VMEM((T, H), bf16),
        pltpu.VMEM((T, H), bf16),
        dma((4,)), dma((6,)), dma((6,)), dma((4,)), dma((4,)), dma((2,)), dma((2,)),
    ]
    if with_point:
        scratch += [
            pltpu.VMEM(act_shape, bf16),
            pltpu.VMEM((T, H), bf16),
            pltpu.VMEM((T, H), bf16),
            pltpu.VMEM((C, 2 * T), bf16),
            pltpu.VMEM((nz - 1, tiles, rows, tile), bf16),
            pltpu.VMEM((nz - 1, tiles, rows, tile), bf16),
            dma((tiles,)), dma((tiles,)), dma((nz - 1, tiles)), dma((nz - 1, tiles)),
        ]
    results = pl.pallas_call(
        functools.partial(kernel, n, tile, with_point),
        out_shape=outs,
        in_specs=[vmem, hbm, hbm, vmem],
        out_specs=[vmem] * len(outs),
        scratch_shapes=scratch,
        compiler_params=pltpu.CompilerParams(
            collective_id=0, has_side_effects=True, vmem_limit_bytes=48 * 1024 * 1024
        ),
    )(inputs, jnp.transpose(w_dilated, (1, 0, 2)), w_point, cotangent)
    if with_point:
        return tuple(results)
    output, grad_inputs, act, full_grad = results
    activation = jnp.transpose(act, (1, 0, 2)).reshape(T, H)
    grad_point = lax.psum_scatter(
        jnp.einsum("to,tc->oc", full_grad, activation, preferred_element_type=f32),
        "seq",
        scatter_dimension=0,
        tiled=True,
    )
    return (output, grad_inputs, grad_point)


def solution(mesh):
    placed = (
        P(("groups", "seq"), "tensor"),
        P(None, None, "tensor"),
        P(None, "tensor"),
        P(("groups", "seq"), "tensor"),
    )
    return jax.shard_map(
        functools.partial(local, mesh.shape["seq"]),
        mesh=mesh,
        in_specs=placed,
        out_specs=(
            P(("groups", "seq"), "tensor"),
            P(("groups", "seq"), "tensor"),
            P(("groups", "seq"), "tensor"),
        ),
        check_vma=False,
    )
```

```python
import functools
import math

import jax
import jax.numpy as jnp
from jax import lax
from jax.experimental import pallas as pl
from jax.experimental.pallas import tpu as pltpu
from jax.sharding import PartitionSpec as P

DILATION_BINS = 32
MESH = pl.DeviceIdType.MESH

gelu_cubic = 0.044715
gelu_scale = math.sqrt(2.0 / math.pi)


def gelu_pair(values):
    square = values * values
    tangent = jnp.tanh(gelu_scale * (values + gelu_cubic * square * values))
    half = 0.5 * (1.0 + tangent)
    slope = half + 0.5 * values * (1.0 - tangent * tangent) * gelu_scale * (
        1.0 + 3.0 * gelu_cubic * square
    )
    return values * half, slope


def dot_nn(a, b):
    return jnp.dot(a, b, preferred_element_type=jnp.float32)


def dot_nt(a, b):
    return lax.dot_general(a, b, (((1,), (1,)), ((), ())), preferred_element_type=jnp.float32)


def kernel(n, tile, with_point, *refs):
    x_ref, w_hbm, p_hbm, d_ref = refs[:4]
    if with_point:
        out_ref, gi_ref, gp_ref = refs[4:7]
        act, dfull = refs[7:9]
        rest = refs[9:]
    else:
        out_ref, gi_ref, act, dfull = refs[4:8]
        rest = refs[8:]
    (w, p, xfull, slope, ghpad, msend, mrecv, bsend, brecv) = rest[:9]
    (lsem, ssem, rsem, xs_sem, xr_sem, gs_sem, gr_sem) = rest[9:16]
    if with_point:
        (actp, dp, dps, cot_t, gps, gpr, as_sem, ar_sem, ps_sem, pr_sem) = rest[16:]

    s = lax.axis_index("seq")
    t = lax.axis_index("tensor")
    o = 1 - t
    T, H = x_ref.shape
    C = 2 * H
    R = DILATION_BINS
    tiles = H // tile
    bf16 = jnp.bfloat16
    has_low = s > 0
    has_high = s < n - 1
    mine = pl.ds(pl.multiple_of(t * H, H), H)
    other = pl.ds(pl.multiple_of(o * H, H), H)
    nz = n // 2
    z = s // 2
    y = lax.rem(s, 2)
    pair = s + 1 - 2 * y

    def remote(src, dst, send, recv, seq, tensor):
        return pltpu.make_async_remote_copy(
            src_ref=src,
            dst_ref=dst,
            send_sem=send,
            recv_sem=recv,
            device_id={"seq": seq, "tensor": tensor},
            device_id_type=MESH,
        )

    def cols(j):
        return pl.ds(pl.multiple_of(j * tile, tile), tile)

    w_loads = [pltpu.make_async_copy(w_hbm.at[k], w.at[k], lsem.at[k]) for k in range(3)]
    p_load = pltpu.make_async_copy(p_hbm, p, lsem.at[3])
    for load in w_loads:
        load.start()
    p_load.start()

    barrier = pltpu.get_barrier_semaphore()

    def greet(seq, tensor):
        pl.semaphore_signal(
            barrier, inc=1, device_id={"seq": seq, "tensor": tensor}, device_id_type=MESH
        )

    greet(s, o)

    @pl.when(has_low)
    def _():
        greet(s - 1, t)
        greet(s - 1, o)

    @pl.when(has_high)
    def _():
        greet(s + 1, t)
        greet(s + 1, o)

    if with_point:
        for d in range(1, nz):
            greet(lax.rem(z + d, nz) * 2 + y, t)
    xfull[pl.ds(R, T), mine] = x_ref[...]
    dfull[:, mine] = d_ref[...]
    sides = lax.div(s + n - 1, n) + lax.div(2 * n - 2 - s, n)
    pl.semaphore_wait(barrier, 1 + (nz - 1 if with_point else 0) + 2 * sides)

    def to_low(slot, tensor):
        return remote(
            x_ref.at[pl.ds(0, R), :], xfull.at[pl.ds(R + T, R), mine],
            xs_sem.at[slot], xr_sem.at[2 + t], s - 1, tensor,
        )

    def to_high(slot, tensor):
        return remote(
            x_ref.at[pl.ds(T - R, R), :], xfull.at[pl.ds(0, R), mine],
            xs_sem.at[2 + slot], xr_sem.at[t], s + 1, tensor,
        )

    @pl.when(has_low)
    def _():
        to_low(0, t).start()
        to_low(1, o).start()

    @pl.when(has_high)
    def _():
        to_high(0, t).start()
        to_high(1, o).start()

    x_side = remote(x_ref, xfull.at[pl.ds(R, T), mine], ssem.at[0], rsem.at[0], s, o)
    x_side.start()
    d_side = remote(d_ref, dfull.at[:, mine], ssem.at[1], rsem.at[1], s, o)
    d_side.start()
    if with_point:
        d_pair = remote(d_ref, dp, ssem.at[2], rsem.at[2], pair, t)
        d_pair.start()
        d_next = remote(dp, dps, ssem.at[3], rsem.at[3], s, o)
        cot_t[mine, pl.ds(0, T)] = d_ref[...].T

    @pl.when(s == 0)
    def _():
        xfull[pl.ds(0, R), :] = jnp.zeros((R, C), bf16)
        ghpad[pl.ds(0, R), :] = jnp.zeros((R, H), bf16)

    @pl.when(s == n - 1)
    def _():
        xfull[pl.ds(R + T, R), :] = jnp.zeros((R, C), bf16)
        ghpad[pl.ds(R + T, R), :] = jnp.zeros((R, H), bf16)

    remote(x_ref, xfull.at[pl.ds(R, T), other], ssem.at[0], rsem.at[0], s, o).wait_recv()

    @pl.when(has_low)
    def _():
        for half in range(2):
            remote(
                x_ref.at[pl.ds(0, R), :], xfull.at[pl.ds(0, R), pl.ds(half * H, H)],
                xs_sem.at[0], xr_sem.at[half], s - 1, t,
            ).wait_recv()

    @pl.when(has_high)
    def _():
        for half in range(2):
            remote(
                x_ref.at[pl.ds(0, R), :], xfull.at[pl.ds(R + T, R), pl.ds(half * H, H)],
                xs_sem.at[0], xr_sem.at[2 + half], s + 1, t,
            ).wait_recv()

    for load in w_loads:
        load.wait()

    def act_copy(j):
        return remote(
            act.at[j], actp.at[j], as_sem.at[j], ar_sem.at[j], pair, t
        )

    @pl.loop(0, tiles)
    def _(j):
        hidden = dot_nn(xfull[pl.ds(0, T), :], w[0, :, cols(j)])
        hidden += dot_nn(xfull[pl.ds(R, T), :], w[1, :, cols(j)])
        hidden += dot_nn(xfull[pl.ds(2 * R, T), :], w[2, :, cols(j)])
        value, derivative = gelu_pair(hidden)
        act[j] = value.astype(bf16)
        slope[:, cols(j)] = derivative
        if with_point:
            act_copy(j).start()

    if with_point:
        remote(d_ref, dp, ssem.at[2], rsem.at[2], pair, t).wait_recv()
        d_next.start()
        cot_t[mine, pl.ds(T, T)] = dp[...].T
    remote(d_ref, dfull.at[:, other], ssem.at[1], rsem.at[1], s, o).wait_recv()
    p_load.wait()
    if with_point:
        cot_t[other, pl.ds(0, T)] = dfull[:, other].T

    @pl.loop(0, tiles)
    def _(j):
        grad = dot_nn(dfull[...], p[:, cols(j)]) * slope[:, cols(j)]
        ghpad[pl.ds(R, T), cols(j)] = grad.astype(bf16)

    gh_low = remote(
        ghpad.at[pl.ds(R, R), :], ghpad.at[pl.ds(R + T, R), :],
        gs_sem.at[0], gr_sem.at[1], s - 1, t,
    )
    gh_high = remote(
        ghpad.at[pl.ds(T, R), :], ghpad.at[pl.ds(0, R), :],
        gs_sem.at[1], gr_sem.at[0], s + 1, t,
    )

    @pl.when(has_low)
    def _():
        gh_low.start()

    @pl.when(has_high)
    def _():
        gh_high.start()

    def point_copy(d, j):
        return remote(
            gps.at[d - 1, j], gpr.at[d - 1, j], ps_sem.at[d - 1, j], pr_sem.at[d - 1, j],
            lax.rem(z + d, nz) * 2 + y, t,
        )

    if with_point:
        rows = gp_ref.shape[0]
        remote(dp, dps, ssem.at[3], rsem.at[3], s, o).wait_recv()
        cot_t[other, pl.ds(T, T)] = dps[...].T

        @pl.loop(0, tiles)
        def _(j):
            act_copy(j).wait_recv()

            def block(d):
                owner = lax.rem(z + d, nz) * 2 + y
                at = pl.ds(pl.multiple_of(owner * rows, rows), rows)
                return dot_nn(cot_t[at, pl.ds(0, T)], act[j]) + dot_nn(
                    cot_t[at, pl.ds(T, T)], actp[j]
                )

            for d in range(1, nz):
                gps[d - 1, j] = block(d).astype(bf16)
                point_copy(d, j).start()
            gp_ref[:, cols(j)] = block(0)

    def mixed(at):
        total = dot_nt(act[0], p[at, pl.ds(0, tile)])
        for i in range(1, tiles):
            total += dot_nt(act[i], p[at, pl.ds(i * tile, tile)])
        return total.astype(bf16)

    @pl.loop(0, tiles)
    def _(j):
        msend[:, cols(j)] = mixed(pl.ds(pl.multiple_of(o * H + j * tile, tile), tile))

    m_side = remote(msend, mrecv, ssem.at[4], rsem.at[4], s, o)
    m_side.start()

    @pl.when(has_low)
    def _():
        remote(
            ghpad.at[pl.ds(R, R), :], ghpad.at[pl.ds(0, R), :],
            gs_sem.at[0], gr_sem.at[0], s - 1, t,
        ).wait_recv()

    @pl.when(has_high)
    def _():
        remote(
            ghpad.at[pl.ds(R, R), :], ghpad.at[pl.ds(R + T, R), :],
            gs_sem.at[0], gr_sem.at[1], s + 1, t,
        ).wait_recv()

    def back(at):
        total = dot_nt(ghpad[pl.ds(2 * R, T), :], w[0, at, :])
        total += dot_nt(ghpad[pl.ds(R, T), :], w[1, at, :])
        total += dot_nt(ghpad[pl.ds(0, T), :], w[2, at, :])
        return total.astype(bf16)

    @pl.loop(0, tiles)
    def _(j):
        bsend[:, cols(j)] = back(pl.ds(pl.multiple_of(o * H + j * tile, tile), tile))

    b_side = remote(bsend, brecv, ssem.at[5], rsem.at[5], s, o)
    b_side.start()
    m_side.wait_recv()

    @pl.loop(0, tiles)
    def _(j):
        own = mixed(pl.ds(pl.multiple_of(t * H + j * tile, tile), tile))
        total = x_ref[:, cols(j)].astype(jnp.float32) + own.astype(jnp.float32)
        out_ref[:, cols(j)] = (total + mrecv[:, cols(j)].astype(jnp.float32)).astype(bf16)

    b_side.wait_recv()

    @pl.loop(0, tiles)
    def _(j):
        own = back(pl.ds(pl.multiple_of(t * H + j * tile, tile), tile))
        total = d_ref[:, cols(j)].astype(jnp.float32) + own.astype(jnp.float32)
        gi_ref[:, cols(j)] = (total + brecv[:, cols(j)].astype(jnp.float32)).astype(bf16)

    if with_point:

        @pl.loop(0, tiles)
        def _(j):
            total = gp_ref[:, cols(j)]
            for d in range(1, nz):
                point_copy(d, j).wait_recv()
                total += gpr[d - 1, j].astype(jnp.float32)
            gp_ref[:, cols(j)] = total

    @pl.when(has_low)
    def _():
        to_low(0, t).wait_send()
        to_low(1, o).wait_send()
        gh_low.wait_send()

    @pl.when(has_high)
    def _():
        to_high(0, t).wait_send()
        to_high(1, o).wait_send()
        gh_high.wait_send()

    x_side.wait_send()
    d_side.wait_send()
    m_side.wait_send()
    b_side.wait_send()
    if with_point:
        d_pair.wait_send()
        d_next.wait_send()

        @pl.loop(0, tiles)
        def _(j):
            act_copy(j).wait_send()
            for d in range(1, nz):
                point_copy(d, j).wait_send()


def kernel8(tile, ahead, *refs):
    x_hbm, w_hbm, p_hbm, d_hbm, out_ref, gi_ref, gp_ref = refs[:7]
    (w, p, xpad, rim, hid, slope, act, actp, d, dt, ct, ghpad) = refs[7:19]
    (msend, mrecv, bsend, brecv, gps, gpa, gpb) = refs[19:26]
    (load, x_s, x_r, d_s, d_r, rim_s, rim_r, rimf_s, rimf_r, co_s, co_r) = refs[26:37]
    (cp_s, cp_r, cf_s, cf_r, a_s, a_r, gh_s, gh_r, m_s, m_r, b_s, b_r) = refs[37:49]
    (z_s, za_r, zb_r, cte, ae) = refs[49:54]
    (am_s, am_r, eo_s, eo_r, ef_s, ef_r, ae_s, ae_r, aef_s, aef_r) = refs[54:]

    s = lax.axis_index("seq")
    t = lax.axis_index("tensor")
    o = 1 - t
    z = s // 2
    y = lax.rem(s, 2)
    pair = s + 1 - 2 * y
    T, H = out_ref.shape
    R = DILATION_BINS
    rows = gp_ref.shape[0]
    tiles = H // tile
    chunks, wide = act.shape[0], act.shape[2]
    per = tile // wide
    bf16, f32 = jnp.bfloat16, jnp.float32
    low = s > 0
    high = s < 7
    outer = lax.rem(z + 1, 4) < 2
    inner = lax.rem(z + 1, 4) >= 2
    upper = z // 2
    far_outer = 3 - 3 * upper
    far_inner = 2 - upper
    near_inner = 1 + upper
    near_outer = 3 * upper
    early = 1 - upper
    next_one, last_one = jnp.where(outer, early, upper), jnp.where(outer, upper, early)
    beside = jnp.where(outer, near_inner, near_outer)

    def remote(src, dst, send, recv, seq, tensor):
        return pltpu.make_async_remote_copy(
            src_ref=src, dst_ref=dst, send_sem=send, recv_sem=recv,
            device_id={"seq": seq, "tensor": tensor}, device_id_type=MESH,
        )

    def cols(j):
        return pl.ds(pl.multiple_of(j * tile, tile), tile)

    barrier = pltpu.get_barrier_semaphore()

    def greet(seq, tensor):
        pl.semaphore_signal(
            barrier, inc=1, device_id={"seq": seq, "tensor": tensor}, device_id_type=MESH
        )

    greet(pair, t)

    @pl.when(z > 0)
    def _():
        greet(s - 2, t)

    @pl.when(z < 3)
    def _():
        greet(s + 2, t)

    @pl.when(jnp.logical_and(y == 0, z > 0))
    def _():
        greet(s - 1, t)

    @pl.when(jnp.logical_and(y == 1, z < 3))
    def _():
        greet(s + 1, t)

    @pl.when(y == lax.rem(z, 2))
    def _():
        greet(2 * beside + 1 - y, t)

    greet(s, o)

    own = pl.ds(pl.multiple_of(t * H, H), H)
    other = pl.ds(pl.multiple_of(o * H, H), H)
    body = pl.ds(R, T)
    x_load = pltpu.make_async_copy(x_hbm, xpad.at[t, body], load.at[0])
    d_load = pltpu.make_async_copy(d_hbm, d.at[t], load.at[1])
    w_own = [
        pltpu.make_async_copy(w_hbm.at[k, own], w.at[k, own], load.at[2 + k]) for k in range(3)
    ]
    w_other = [
        pltpu.make_async_copy(w_hbm.at[k, other], w.at[k, other], load.at[5 + k])
        for k in range(3)
    ]
    p_load = pltpu.make_async_copy(p_hbm, p, load.at[8])
    for copy in [d_load, x_load] + w_own + w_other + [p_load]:
        copy.start()

    for half in range(2):
        xpad[half, pl.ds(0, R)] = jnp.zeros((R, H), bf16)
        xpad[half, pl.ds(R + T, R)] = jnp.zeros((R, H), bf16)

    @pl.when(s == 0)
    def _():
        rim[0] = jnp.zeros((2, R, H), bf16)
        ghpad[pl.ds(0, R), :] = jnp.zeros((R, H), bf16)

    @pl.when(s == 7)
    def _():
        rim[1] = jnp.zeros((2, R, H), bf16)
        ghpad[pl.ds(R + T, R), :] = jnp.zeros((R, H), bf16)

    d_load.wait()
    dt[...] = d[t].T

    def dt_block(i, side):
        return pl.ds(pl.multiple_of((2 * i + side) * rows, rows), rows)

    for i in range(2):
        ct[2 * t + i, 0] = dt[dt_block(i, y), :]

    x_load.wait()
    for copy in w_own:
        copy.wait()

    def taps(half, rows_of, j):
        total = dot_nn(xpad[half, pl.ds(0, T)], w[0, rows_of, cols(j)])
        total += dot_nn(xpad[half, pl.ds(R, T)], w[1, rows_of, cols(j)])
        return total + dot_nn(xpad[half, pl.ds(2 * R, T)], w[2, rows_of, cols(j)])

    @pl.loop(0, tiles)
    def _(j):
        hid[:, cols(j)] = taps(t, own, j)

    met = 2 + jnp.where(z > 0, 1, 0) + jnp.where(z < 3, 1, 0) + jnp.where(y == lax.rem(z, 2), 1, 0)
    pl.semaphore_wait(barrier, met + jnp.where(jnp.where(y == 0, z > 0, z < 3), 1, 0))

    to_low = remote(
        xpad.at[t, pl.ds(R, R)], rim.at[1, t], rim_s.at[0], rim_r.at[1], s - 1, t
    )
    to_high = remote(
        xpad.at[t, pl.ds(T, R)], rim.at[0, t], rim_s.at[1], rim_r.at[0], s + 1, t
    )

    def when_low(act_on):
        pl.when(low)(act_on)

    def when_high(act_on):
        pl.when(high)(act_on)

    pl.when(jnp.logical_and(y == 0, low))(to_low.start)
    when_high(to_high.start)
    pl.when(jnp.logical_and(y == 1, low))(to_low.start)
    x_side = remote(xpad.at[t, body], xpad.at[t, body], x_s, x_r, s, o)
    x_side.start()

    def cot_pair(i):
        return remote(
            dt.at[dt_block(i, 1 - y), :], ct.at[2 * t + i, 1], cp_s.at[i], cp_r.at[i], pair, t
        )

    def cot_on(i, half):
        return remote(
            ct.at[2 * t + i, 1], ct.at[2 * half + i, 1], cf_s.at[i], cf_r.at[i], s, o
        )

    cot_own = [
        remote(ct.at[2 * t + i, 0], ct.at[2 * t + i, 0], co_s.at[i], co_r.at[i], s, o)
        for i in range(2)
    ]

    def each(copies, what):
        def run():
            for copy in copies:
                getattr(copy, what)()
        return run

    pl.when(t == early)(cot_pair(early).start)

    def cot_ahead(i, side):
        return remote(
            dt.at[dt_block(i, (y if side == 0 else 1 - y)), :], cte.at[2 * t + i, side],
            eo_s.at[i, side], eo_r.at[i, side], 2 * near_inner + (y if side == 0 else 1 - y), t,
        )

    def cot_ahead_on(i, side, half):
        return remote(
            cte.at[2 * t + i, side], cte.at[2 * half + i, side],
            ef_s.at[i, side], ef_r.at[i, side], s, o,
        )

    sends_ahead = jnp.logical_and(outer, ahead > 0)
    takes_ahead = jnp.logical_and(inner, ahead > 0)

    @pl.when(jnp.logical_and(sends_ahead, t == early))
    def _():
        for i in range(2):
            for side in range(2):
                cot_ahead(i, side).start()

    d_side = remote(d.at[t], d.at[t], d_s, d_r, s, o)
    d_side.start()
    each(cot_own, "start")()

    remote(xpad.at[t, body], xpad.at[o, body], x_s, x_r, s, o).wait_recv()
    for copy in w_other:
        copy.wait()

    def act_copy(c):
        return remote(act.at[c], actp.at[c], a_s.at[c], a_r.at[c], pair, t)

    edges = (pl.ds(R, T - 2 * R), pl.ds(0, R), pl.ds(T - R, R))

    def act_part(c, k):
        return remote(
            act.at[c, edges[k]], actp.at[c, edges[k]], am_s.at[c, k], am_r.at[c, k], pair, t
        )

    def act_copies(c):
        return [act_part(c, k) for k in range(3)] if c < per else [act_copy(c)]

    def activate(j, rows_of):
        value, derivative = gelu_pair(hid[rows_of, cols(j)])
        value = value.astype(bf16)
        for i in range(per):
            act[per * j + i, rows_of] = value[:, i * wide:(i + 1) * wide]
        slope[rows_of, cols(j)] = derivative

    first_sent = [c for c in range(ahead, per)] + [c for c in range(min(ahead, per))]

    def middle_rows(j):
        hid[:, cols(j)] += taps(o, other, j)
        activate(j, edges[0])

    middle_rows(0)
    act_part(first_sent[0], 0).start()
    pl.when(t == early)(cot_pair(1 - early).start)
    pl.when(jnp.logical_and(t != early, inner))(cot_pair(next_one).start)

    @pl.loop(1, tiles)
    def _(j):
        middle_rows(j)

    def rim_on(k):
        return remote(rim.at[k, t], rim.at[k, t], rimf_s.at[k], rimf_r.at[k], s, o)

    def rim_land(k):
        remote(xpad.at[t, pl.ds(R, R)], rim.at[k, t], rim_s.at[0], rim_r.at[k], s, o).wait_recv()
        rim_on(k).start()

    def rim_land_on(k):
        remote(rim.at[k, t], rim.at[k, o], rimf_s.at[k], rimf_r.at[k], s, o).wait_recv()

    when_low(functools.partial(rim_land, 0))
    when_high(functools.partial(rim_land, 1))
    when_low(functools.partial(rim_land_on, 0))
    when_high(functools.partial(rim_land_on, 1))

    def edge_rows(j):
        at = cols(j)
        first = dot_nn(rim[0, 0], w[0, pl.ds(0, H), at]) + dot_nn(rim[0, 1], w[0, pl.ds(H, H), at])
        last = dot_nn(rim[1, 0], w[2, pl.ds(0, H), at]) + dot_nn(rim[1, 1], w[2, pl.ds(H, H), at])
        hid[edges[1], at] += first
        hid[edges[2], at] += last
        activate(j, edges[1])
        activate(j, edges[2])

    def act_ahead(c):
        return remote(
            act.at[c], ae.at[0, c], ae_s.at[c], ae_r.at[c], 2 * near_inner + y, t
        )

    def act_ahead_on(c):
        return remote(ae.at[0, c], ae.at[1, c], aef_s.at[c], aef_r.at[c], pair, t)

    edge_rows(0)
    act_part(first_sent[0], 1).start()
    act_part(first_sent[0], 2).start()
    soon = [c for c in first_sent[1:] if c >= ahead]
    last_sent = [c for c in first_sent[1:] if c < ahead]
    for c in soon:
        for k in range(3):
            act_part(c, k).start()

    @pl.when(outer)
    def _():
        for c in range(ahead):
            act_ahead(c).start()

    def last_parts():
        pl.when(t != early)(cot_pair(last_one).start)
        for c in last_sent:
            for k in range(3):
                act_part(c, k).start()

    for j in range(1, tiles):
        edge_rows(j)
        for c in range(per * j, per * j + per):
            act_copy(c).start()

    pl.when(jnp.logical_and(t != early, outer))(cot_pair(next_one).start)

    def cot_land(i):
        cot_pair(i).wait_recv()
        cot_on(i, t).start()

    def cot_land_late(i):
        @pl.when(t != early)
        def _():
            cot_land(i)

    def cot_land_late_on(i):
        @pl.when(t == early)
        def _():
            cot_on(i, o).wait_recv()

    pl.when(t == early)(functools.partial(cot_land, early))

    remote(d.at[t], d.at[o], d_s, d_r, s, o).wait_recv()
    p_load.wait()

    @pl.loop(0, tiles)
    def _(j):
        grad = dot_nn(d[0], p[pl.ds(0, H), cols(j)]) + dot_nn(d[1], p[pl.ds(H, H), cols(j)])
        ghpad[pl.ds(R, T), cols(j)] = (grad * slope[:, cols(j)]).astype(bf16)

    gh_low = remote(
        ghpad.at[pl.ds(R, R), :], ghpad.at[pl.ds(R + T, R), :], gh_s.at[0], gh_r.at[1], s - 1, t
    )
    gh_high = remote(
        ghpad.at[pl.ds(T, R), :], ghpad.at[pl.ds(0, R), :], gh_s.at[1], gh_r.at[0], s + 1, t
    )

    def gh_send():
        when_low(gh_low.start)
        when_high(gh_high.start)


    def act_tile(i):
        return jnp.concatenate([act[per * i + k] for k in range(per)], axis=1)

    def mixed(at):
        total = dot_nt(act_tile(0), p[at, pl.ds(0, tile)])
        for i in range(1, tiles):
            total += dot_nt(act_tile(i), p[at, pl.ds(i * tile, tile)])
        return total.astype(bf16)

    def back(at):
        total = dot_nt(ghpad[pl.ds(2 * R, T), :], w[0, at, :])
        total += dot_nt(ghpad[pl.ds(R, T), :], w[1, at, :])
        total += dot_nt(ghpad[pl.ds(0, T), :], w[2, at, :])
        return total.astype(bf16)

    def rows_at(half, j):
        return pl.ds(pl.multiple_of(half * H + j * tile, tile), tile)

    m_side = remote(msend, mrecv, m_s, m_r, s, o)
    b_side = remote(bsend, brecv, b_s, b_r, s, o)

    def mixed_other():
        @pl.loop(0, tiles)
        def _(j):
            msend[:, cols(j)] = mixed(rows_at(o, j))
        m_side.start()

    def mixed_own():
        m_side.wait_recv()

        @pl.loop(0, tiles)
        def _(j):
            total = xpad[t, body, cols(j)].astype(f32) + mixed(rows_at(t, j)).astype(f32)
            out_ref[:, cols(j)] = (total + mrecv[:, cols(j)].astype(f32)).astype(bf16)

    def back_other(first, last):
        @pl.loop(first, last)
        def _(j):
            bsend[:, cols(j)] = back(rows_at(o, j))

    def back_own(first, last):
        @pl.loop(first, last)
        def _(j):
            total = d[t, :, cols(j)].astype(f32) + back(rows_at(t, j)).astype(f32)
            gi_ref[:, cols(j)] = (total + brecv[:, cols(j)].astype(f32)).astype(bf16)

    def gh_land():
        def land(k):
            remote(
                ghpad.at[pl.ds(R, R), :], ghpad.at[pl.ds(k * (R + T), R), :],
                gh_s.at[0], gh_r.at[k], s, o,
            ).wait_recv()
        when_low(functools.partial(land, 0))
        when_high(functools.partial(land, 1))

    def block(zd, c):
        return dot_nn(ct[zd, 0], act[c]) + dot_nn(ct[zd, 1], actp[c])

    def block_ahead(zd, c):
        return dot_nn(cte[zd, 0], ae[0, c]) + dot_nn(cte[zd, 1], ae[1, c])

    def to_a(k, c, zt):
        return remote(gps.at[k, c], gpa.at[k, c], z_s.at[k, c], za_r.at[k, c], 2 * zt + y, t)

    def to_end(c, zt):
        return remote(gps.at[2, c], gpa.at[0, c], z_s.at[2, c], za_r.at[0, c], 2 * zt + y, t)

    def to_b(k, c, zt):
        return remote(gps.at[k, c], gpb.at[k, c], z_s.at[k, c], zb_r.at[k, c], 2 * zt + y, t)

    def act_land(c):
        for copy in act_copies(c):
            copy.wait_recv()

    def feed(k, c):
        zd = (far_outer, far_inner, near_inner)[k]
        gps[k, c] = block(zd, c).astype(bf16)
        to_a(k, c, near_inner).start()

    def ahead_land():
        @pl.when(t == early)
        def _():
            for i in range(2):
                for side in range(2):
                    cot_ahead(i, side).wait_recv()
                    cot_ahead_on(i, side, t).start()

    def act_ahead_land():
        for c in range(ahead):
            act_ahead(c).wait_recv()
            act_ahead_on(c).start()

    def ahead_land_on():
        @pl.when(t != early)
        def _():
            for i in range(2):
                for side in range(2):
                    cot_ahead_on(i, side, o).wait_recv()
        for c in range(ahead):
            act_ahead_on(c).wait_recv()

    def middle_ahead(c):
        for k, zd in ((0, far_outer), (1, far_inner)):
            gps[k, c] = (block(zd, c) + block_ahead(zd, c)).astype(bf16)
            to_b(k, c, far_inner).start()

    def middle(k, c):
        part = block((far_outer, far_inner)[k], c)
        to_a(k, c, near_inner).wait_recv()
        gps[k, c] = (part + gpa[k, c].astype(f32)).astype(bf16)
        to_b(k, c, far_inner).start()

    def back_to_end(c):
        part = block(near_outer, c)
        to_b(0, c, far_inner).wait_recv()
        gps[2, c] = (part + gpb[0, c].astype(f32)).astype(bf16)
        to_end(c, near_outer).start()

    def chunk_cols(c):
        return pl.ds(pl.multiple_of(c * wide, wide), wide)

    def own_block(c):
        gp_ref[:, chunk_cols(c)] = block(z, c)

    @pl.when(t != early)
    def _():
        cot_on(early, o).wait_recv()

    @pl.when(t == early)
    def _():
        cot_land(1 - early)

    for i in range(2):
        remote(ct.at[2 * t + i, 0], ct.at[2 * o + i, 0], co_s.at[i], co_r.at[i], s, o).wait_recv()

    def far_inner_ready():
        @pl.when(t != early)
        def _():
            cot_on(1 - early, o).wait_recv()

    def back_first():
        gh_land()
        back_other(0, tiles)
        b_side.start()

    def own_blocks():
        for c in range(chunks):
            own_block(c)

    def back_last():
        b_side.wait_recv()
        back_own(0, tiles)

    rest = list(range(ahead, chunks))

    gh_send()

    @pl.when(outer)
    def _():
        last_parts()
        act_land(rest[0])
        feed(0, rest[0])
        mixed_other()
        far_inner_ready()
        act_land(rest[1])
        feed(0, rest[1])
        feed(1, rest[0])
        mixed_own()
        for i in range(2, len(rest)):
            act_land(rest[i])
            feed(0, rest[i])
            feed(1, rest[i - 1])
        feed(1, rest[-1])
        cot_land_late(next_one)
        cot_land_late_on(next_one)
        for c in rest:
            feed(2, c)
        for c in range(ahead):
            act_land(c)
            feed(2, c)
        back_first()
        cot_land_late(last_one)
        cot_land_late_on(last_one)
        own_blocks()
        back_last()

    @pl.when(inner)
    def _():
        mixed_other()
        far_inner_ready()
        if ahead:
            ahead_land()
        mixed_own()
        act_ahead_land()
        last_parts()
        cot_land_late(next_one)
        act_land(rest[0])
        middle(0, rest[0])
        cot_land_late_on(next_one)
        for i in range(1, len(rest)):
            act_land(rest[i])
            middle(0, rest[i])
            if i > 1:
                back_to_end(rest[i - 2])
            middle(1, rest[i - 1])
        back_to_end(rest[-2])
        back_first()
        middle(1, rest[-1])
        back_to_end(rest[-1])
        if ahead:
            for c in range(ahead):
                act_land(c)
            ahead_land_on()
            for c in range(ahead):
                middle_ahead(c)
        cot_land_late(last_one)
        cot_land_late_on(last_one)
        own_blocks()
        for c in range(ahead):
            back_to_end(c)
        back_last()

    for c in rest + list(range(ahead)):
        @pl.when(outer)
        def _():
            to_end(c, near_outer).wait_recv()
            gp_ref[:, chunk_cols(c)] += gpa[0, c].astype(f32)

        @pl.when(inner)
        def _():
            to_b(1, c, far_inner).wait_recv()
            part = gp_ref[:, chunk_cols(c)] + gpb[1, c].astype(f32)
            to_a(2, c, near_inner).wait_recv()
            gp_ref[:, chunk_cols(c)] = part + gpa[2, c].astype(f32)

    when_low(to_low.wait_send)
    when_high(to_high.wait_send)
    when_low(rim_on(0).wait_send)
    when_high(rim_on(1).wait_send)
    when_low(gh_low.wait_send)
    when_high(gh_high.wait_send)
    for copy in [x_side, d_side, m_side, b_side] + cot_own:
        copy.wait_send()
    for i in range(2):
        cot_pair(i).wait_send()
        cot_on(i, t).wait_send()
    for c in range(chunks):
        for copy in act_copies(c):
            copy.wait_send()
        if c >= ahead:
            for k in range(3):
                to_a(k, c, near_inner).wait_send()

    @pl.when(sends_ahead)
    def _():
        @pl.when(t == early)
        def _():
            for i in range(2):
                for side in range(2):
                    cot_ahead(i, side).wait_send()
        for c in range(ahead):
            act_ahead(c).wait_send()
            to_a(2, c, near_inner).wait_send()

    @pl.when(takes_ahead)
    def _():
        @pl.when(t == early)
        def _():
            for i in range(2):
                for side in range(2):
                    cot_ahead_on(i, side, t).wait_send()
        for c in range(ahead):
            act_ahead_on(c).wait_send()
            for k in range(3):
                to_a(k, c, near_inner).wait_send()


def writer(out_ref, gi_ref, gp_ref, out_hbm, gi_hbm, gp_hbm, sem):
    copies = [
        pltpu.make_async_copy(src, dst, sem.at[i])
        for i, (src, dst) in enumerate(
            ((gp_ref, gp_hbm), (out_ref, out_hbm), (gi_ref, gi_hbm))
        )
    ]
    for copy in copies:
        copy.start()
    for copy in copies:
        copy.wait()


def local8(inputs, w_dilated, w_point, cotangent):
    T, H = inputs.shape
    C = w_point.shape[0]
    R = DILATION_BINS
    tile, wide, ahead = 256, 128, 0
    tiles, chunks = H // tile, H // wide
    rows = C // 8
    bf16, f32 = jnp.bfloat16, jnp.float32
    dma = pltpu.SemaphoreType.DMA
    vmem = pl.BlockSpec(memory_space=pltpu.VMEM)
    hbm = pl.BlockSpec(memory_space=pltpu.HBM)
    shapes = [
        ((3, C, H), bf16), ((C, H), bf16), ((2, T + 2 * R, H), bf16), ((2, 2, R, H), bf16),
        ((T, H), f32), ((T, H), f32), ((chunks, T, wide), bf16), ((chunks, T, wide), bf16),
        ((2, T, H), bf16), ((H, T), bf16), ((4, 2, rows, T), bf16), ((T + 2 * R, H), bf16),
        ((T, H), bf16), ((T, H), bf16), ((T, H), bf16), ((T, H), bf16),
        ((3, chunks, rows, wide), bf16), ((3, chunks, rows, wide), bf16),
        ((2, chunks, rows, wide), bf16),
    ]
    one = dma(())
    two = dma((2,))
    sems = [
        dma((9,)), one, one, one, one, two, two, two, two, two, two,
        two, two, two, two, dma((chunks,)), dma((chunks,)), two, two, one, one, one, one,
        dma((3, chunks)), dma((3, chunks)), dma((2, chunks)),
    ]
    held = max(ahead, 1)
    late = [
        ((4, 2, rows, T), bf16), ((2, held, T, wide), bf16),
    ]
    late_sems = [
        dma((tile // wide, 3)), dma((tile // wide, 3)), dma((2, 2)), dma((2, 2)), dma((2, 2)),
        dma((2, 2)), dma((held,)), dma((held,)), dma((held,)), dma((held,)),
    ]
    outs = [
        jax.ShapeDtypeStruct((T, H), bf16),
        jax.ShapeDtypeStruct((T, H), bf16),
        jax.ShapeDtypeStruct((rows, H), f32),
    ]
    results = pl.pallas_call(
        functools.partial(kernel8, tile, ahead),
        out_shape=[pltpu.VMEM(out.shape, out.dtype) for out in outs],
        in_specs=[hbm] * 4,
        out_specs=[vmem] * 3,
        scratch_shapes=[pltpu.VMEM(*shape) for shape in shapes] + sems
        + [pltpu.VMEM(*shape) for shape in late] + late_sems,
        compiler_params=pltpu.CompilerParams(
            collective_id=0, has_side_effects=True, vmem_limit_bytes=60 * 1024 * 1024
        ),
    )(inputs, jnp.transpose(w_dilated, (1, 0, 2)), w_point, cotangent)
    return tuple(
        pl.pallas_call(
            writer,
            out_shape=outs,
            in_specs=[vmem] * 3,
            out_specs=[hbm] * 3,
            scratch_shapes=[dma((3,))],
            compiler_params=pltpu.CompilerParams(vmem_limit_bytes=1024 * 1024),
        )(*results)
    )


def local(n, inputs, w_dilated, w_point, cotangent):
    if n == 8 and inputs.shape[0] == 256:
        return local8(inputs, w_dilated, w_point, cotangent)
    T, H = inputs.shape
    C = w_point.shape[0]
    R = DILATION_BINS
    tile = 256
    tiles = H // tile
    rows = C // n
    bf16, f32 = jnp.bfloat16, jnp.float32
    with_point = rows % 16 == 0 and n % 2 == 0
    nz = n // 2
    vmem = pl.BlockSpec(memory_space=pltpu.VMEM)
    hbm = pl.BlockSpec(memory_space=pl.ANY)
    plane = jax.ShapeDtypeStruct((T, H), bf16)
    act_shape = (tiles, T, tile)
    outs = [plane, plane]
    scratch = []
    if with_point:
        outs += [jax.ShapeDtypeStruct((rows, H), f32)]
        scratch += [pltpu.VMEM(act_shape, bf16), pltpu.VMEM((T, C), bf16)]
    else:
        outs += [jax.ShapeDtypeStruct(act_shape, bf16), jax.ShapeDtypeStruct((T, C), bf16)]
    dma = pltpu.SemaphoreType.DMA
    scratch += [
        pltpu.VMEM((3, C, H), bf16),
        pltpu.VMEM((C, H), bf16),
        pltpu.VMEM((T + 2 * R, C), bf16),
        pltpu.VMEM((T, H), f32),
        pltpu.VMEM((T + 2 * R, H), bf16),
        pltpu.VMEM((T, H), bf16),
        pltpu.VMEM((T, H), bf16),
        pltpu.VMEM((T, H), bf16),
        pltpu.VMEM((T, H), bf16),
        dma((4,)), dma((6,)), dma((6,)), dma((4,)), dma((4,)), dma((2,)), dma((2,)),
    ]
    if with_point:
        scratch += [
            pltpu.VMEM(act_shape, bf16),
            pltpu.VMEM((T, H), bf16),
            pltpu.VMEM((T, H), bf16),
            pltpu.VMEM((C, 2 * T), bf16),
            pltpu.VMEM((nz - 1, tiles, rows, tile), bf16),
            pltpu.VMEM((nz - 1, tiles, rows, tile), bf16),
            dma((tiles,)), dma((tiles,)), dma((nz - 1, tiles)), dma((nz - 1, tiles)),
        ]
    results = pl.pallas_call(
        functools.partial(kernel, n, tile, with_point),
        out_shape=outs,
        in_specs=[vmem, hbm, hbm, vmem],
        out_specs=[vmem] * len(outs),
        scratch_shapes=scratch,
        compiler_params=pltpu.CompilerParams(
            collective_id=0, has_side_effects=True, vmem_limit_bytes=48 * 1024 * 1024
        ),
    )(inputs, jnp.transpose(w_dilated, (1, 0, 2)), w_point, cotangent)
    if with_point:
        return tuple(results)
    output, grad_inputs, act, full_grad = results
    activation = jnp.transpose(act, (1, 0, 2)).reshape(T, H)
    grad_point = lax.psum_scatter(
        jnp.einsum("to,tc->oc", full_grad, activation, preferred_element_type=f32),
        "seq",
        scatter_dimension=0,
        tiled=True,
    )
    return (output, grad_inputs, grad_point)


def solution(mesh):
    placed = (
        P(("groups", "seq"), "tensor"),
        P(None, None, "tensor"),
        P(None, "tensor"),
        P(("groups", "seq"), "tensor"),
    )
    return jax.shard_map(
        functools.partial(local, mesh.shape["seq"]),
        mesh=mesh,
        in_specs=placed,
        out_specs=(
            P(("groups", "seq"), "tensor"),
            P(("groups", "seq"), "tensor"),
            P(("groups", "seq"), "tensor"),
        ),
        check_vma=False,
    )
```

```python
import functools
import math

import jax
import jax.numpy as jnp
from jax import lax
from jax.experimental import pallas as pl
from jax.experimental.pallas import tpu as pltpu
from jax.sharding import PartitionSpec as P

DILATION_BINS = 32
MESH = pl.DeviceIdType.MESH

gelu_cubic = 0.044715
gelu_scale = math.sqrt(2.0 / math.pi)


def gelu_pair(values):
    square = values * values
    tangent = jnp.tanh(gelu_scale * (values + gelu_cubic * square * values))
    half = 0.5 * (1.0 + tangent)
    slope = half + 0.5 * values * (1.0 - tangent * tangent) * gelu_scale * (
        1.0 + 3.0 * gelu_cubic * square
    )
    return values * half, slope


def dot_nn(a, b):
    return jnp.dot(a, b, preferred_element_type=jnp.float32)


def dot_nt(a, b):
    return lax.dot_general(a, b, (((1,), (1,)), ((), ())), preferred_element_type=jnp.float32)


def kernel(n, tile, with_point, *refs):
    x_ref, w_hbm, p_hbm, d_ref = refs[:4]
    if with_point:
        out_ref, gi_ref, gp_ref = refs[4:7]
        act, dfull = refs[7:9]
        rest = refs[9:]
    else:
        out_ref, gi_ref, act, dfull = refs[4:8]
        rest = refs[8:]
    (w, p, xfull, slope, ghpad, msend, mrecv, bsend, brecv) = rest[:9]
    (lsem, ssem, rsem, xs_sem, xr_sem, gs_sem, gr_sem) = rest[9:16]
    if with_point:
        (actp, dp, dps, cot_t, gps, gpr, as_sem, ar_sem, ps_sem, pr_sem) = rest[16:]

    s = lax.axis_index("seq")
    t = lax.axis_index("tensor")
    o = 1 - t
    T, H = x_ref.shape
    C = 2 * H
    R = DILATION_BINS
    tiles = H // tile
    bf16 = jnp.bfloat16
    has_low = s > 0
    has_high = s < n - 1
    mine = pl.ds(pl.multiple_of(t * H, H), H)
    other = pl.ds(pl.multiple_of(o * H, H), H)
    nz = n // 2
    z = s // 2
    y = lax.rem(s, 2)
    pair = s + 1 - 2 * y

    def remote(src, dst, send, recv, seq, tensor):
        return pltpu.make_async_remote_copy(
            src_ref=src,
            dst_ref=dst,
            send_sem=send,
            recv_sem=recv,
            device_id={"seq": seq, "tensor": tensor},
            device_id_type=MESH,
        )

    def cols(j):
        return pl.ds(pl.multiple_of(j * tile, tile), tile)

    w_loads = [pltpu.make_async_copy(w_hbm.at[k], w.at[k], lsem.at[k]) for k in range(3)]
    p_load = pltpu.make_async_copy(p_hbm, p, lsem.at[3])
    for load in w_loads:
        load.start()
    p_load.start()

    barrier = pltpu.get_barrier_semaphore()

    def greet(seq, tensor):
        pl.semaphore_signal(
            barrier, inc=1, device_id={"seq": seq, "tensor": tensor}, device_id_type=MESH
        )

    greet(s, o)

    @pl.when(has_low)
    def _():
        greet(s - 1, t)
        greet(s - 1, o)

    @pl.when(has_high)
    def _():
        greet(s + 1, t)
        greet(s + 1, o)

    if with_point:
        for d in range(1, nz):
            greet(lax.rem(z + d, nz) * 2 + y, t)
    xfull[pl.ds(R, T), mine] = x_ref[...]
    dfull[:, mine] = d_ref[...]
    sides = lax.div(s + n - 1, n) + lax.div(2 * n - 2 - s, n)
    pl.semaphore_wait(barrier, 1 + (nz - 1 if with_point else 0) + 2 * sides)

    def to_low(slot, tensor):
        return remote(
            x_ref.at[pl.ds(0, R), :], xfull.at[pl.ds(R + T, R), mine],
            xs_sem.at[slot], xr_sem.at[2 + t], s - 1, tensor,
        )

    def to_high(slot, tensor):
        return remote(
            x_ref.at[pl.ds(T - R, R), :], xfull.at[pl.ds(0, R), mine],
            xs_sem.at[2 + slot], xr_sem.at[t], s + 1, tensor,
        )

    @pl.when(has_low)
    def _():
        to_low(0, t).start()
        to_low(1, o).start()

    @pl.when(has_high)
    def _():
        to_high(0, t).start()
        to_high(1, o).start()

    x_side = remote(x_ref, xfull.at[pl.ds(R, T), mine], ssem.at[0], rsem.at[0], s, o)
    x_side.start()
    d_side = remote(d_ref, dfull.at[:, mine], ssem.at[1], rsem.at[1], s, o)
    d_side.start()
    if with_point:
        d_pair = remote(d_ref, dp, ssem.at[2], rsem.at[2], pair, t)
        d_pair.start()
        d_next = remote(dp, dps, ssem.at[3], rsem.at[3], s, o)
        cot_t[mine, pl.ds(0, T)] = d_ref[...].T

    @pl.when(s == 0)
    def _():
        xfull[pl.ds(0, R), :] = jnp.zeros((R, C), bf16)
        ghpad[pl.ds(0, R), :] = jnp.zeros((R, H), bf16)

    @pl.when(s == n - 1)
    def _():
        xfull[pl.ds(R + T, R), :] = jnp.zeros((R, C), bf16)
        ghpad[pl.ds(R + T, R), :] = jnp.zeros((R, H), bf16)

    remote(x_ref, xfull.at[pl.ds(R, T), other], ssem.at[0], rsem.at[0], s, o).wait_recv()

    @pl.when(has_low)
    def _():
        for half in range(2):
            remote(
                x_ref.at[pl.ds(0, R), :], xfull.at[pl.ds(0, R), pl.ds(half * H, H)],
                xs_sem.at[0], xr_sem.at[half], s - 1, t,
            ).wait_recv()

    @pl.when(has_high)
    def _():
        for half in range(2):
            remote(
                x_ref.at[pl.ds(0, R), :], xfull.at[pl.ds(R + T, R), pl.ds(half * H, H)],
                xs_sem.at[0], xr_sem.at[2 + half], s + 1, t,
            ).wait_recv()

    for load in w_loads:
        load.wait()

    def act_copy(j):
        return remote(
            act.at[j], actp.at[j], as_sem.at[j], ar_sem.at[j], pair, t
        )

    @pl.loop(0, tiles)
    def _(j):
        hidden = dot_nn(xfull[pl.ds(0, T), :], w[0, :, cols(j)])
        hidden += dot_nn(xfull[pl.ds(R, T), :], w[1, :, cols(j)])
        hidden += dot_nn(xfull[pl.ds(2 * R, T), :], w[2, :, cols(j)])
        value, derivative = gelu_pair(hidden)
        act[j] = value.astype(bf16)
        slope[:, cols(j)] = derivative
        if with_point:
            act_copy(j).start()

    if with_point:
        remote(d_ref, dp, ssem.at[2], rsem.at[2], pair, t).wait_recv()
        d_next.start()
        cot_t[mine, pl.ds(T, T)] = dp[...].T
    remote(d_ref, dfull.at[:, other], ssem.at[1], rsem.at[1], s, o).wait_recv()
    p_load.wait()
    if with_point:
        cot_t[other, pl.ds(0, T)] = dfull[:, other].T

    @pl.loop(0, tiles)
    def _(j):
        grad = dot_nn(dfull[...], p[:, cols(j)]) * slope[:, cols(j)]
        ghpad[pl.ds(R, T), cols(j)] = grad.astype(bf16)

    gh_low = remote(
        ghpad.at[pl.ds(R, R), :], ghpad.at[pl.ds(R + T, R), :],
        gs_sem.at[0], gr_sem.at[1], s - 1, t,
    )
    gh_high = remote(
        ghpad.at[pl.ds(T, R), :], ghpad.at[pl.ds(0, R), :],
        gs_sem.at[1], gr_sem.at[0], s + 1, t,
    )

    @pl.when(has_low)
    def _():
        gh_low.start()

    @pl.when(has_high)
    def _():
        gh_high.start()

    def point_copy(d, j):
        return remote(
            gps.at[d - 1, j], gpr.at[d - 1, j], ps_sem.at[d - 1, j], pr_sem.at[d - 1, j],
            lax.rem(z + d, nz) * 2 + y, t,
        )

    if with_point:
        rows = gp_ref.shape[0]
        remote(dp, dps, ssem.at[3], rsem.at[3], s, o).wait_recv()
        cot_t[other, pl.ds(T, T)] = dps[...].T

        @pl.loop(0, tiles)
        def _(j):
            act_copy(j).wait_recv()

            def block(d):
                owner = lax.rem(z + d, nz) * 2 + y
                at = pl.ds(pl.multiple_of(owner * rows, rows), rows)
                return dot_nn(cot_t[at, pl.ds(0, T)], act[j]) + dot_nn(
                    cot_t[at, pl.ds(T, T)], actp[j]
                )

            for d in range(1, nz):
                gps[d - 1, j] = block(d).astype(bf16)
                point_copy(d, j).start()
            gp_ref[:, cols(j)] = block(0)

    def mixed(at):
        total = dot_nt(act[0], p[at, pl.ds(0, tile)])
        for i in range(1, tiles):
            total += dot_nt(act[i], p[at, pl.ds(i * tile, tile)])
        return total.astype(bf16)

    @pl.loop(0, tiles)
    def _(j):
        msend[:, cols(j)] = mixed(pl.ds(pl.multiple_of(o * H + j * tile, tile), tile))

    m_side = remote(msend, mrecv, ssem.at[4], rsem.at[4], s, o)
    m_side.start()

    @pl.when(has_low)
    def _():
        remote(
            ghpad.at[pl.ds(R, R), :], ghpad.at[pl.ds(0, R), :],
            gs_sem.at[0], gr_sem.at[0], s - 1, t,
        ).wait_recv()

    @pl.when(has_high)
    def _():
        remote(
            ghpad.at[pl.ds(R, R), :], ghpad.at[pl.ds(R + T, R), :],
            gs_sem.at[0], gr_sem.at[1], s + 1, t,
        ).wait_recv()

    def back(at):
        total = dot_nt(ghpad[pl.ds(2 * R, T), :], w[0, at, :])
        total += dot_nt(ghpad[pl.ds(R, T), :], w[1, at, :])
        total += dot_nt(ghpad[pl.ds(0, T), :], w[2, at, :])
        return total.astype(bf16)

    @pl.loop(0, tiles)
    def _(j):
        bsend[:, cols(j)] = back(pl.ds(pl.multiple_of(o * H + j * tile, tile), tile))

    b_side = remote(bsend, brecv, ssem.at[5], rsem.at[5], s, o)
    b_side.start()
    m_side.wait_recv()

    @pl.loop(0, tiles)
    def _(j):
        own = mixed(pl.ds(pl.multiple_of(t * H + j * tile, tile), tile))
        total = x_ref[:, cols(j)].astype(jnp.float32) + own.astype(jnp.float32)
        out_ref[:, cols(j)] = (total + mrecv[:, cols(j)].astype(jnp.float32)).astype(bf16)

    b_side.wait_recv()

    @pl.loop(0, tiles)
    def _(j):
        own = back(pl.ds(pl.multiple_of(t * H + j * tile, tile), tile))
        total = d_ref[:, cols(j)].astype(jnp.float32) + own.astype(jnp.float32)
        gi_ref[:, cols(j)] = (total + brecv[:, cols(j)].astype(jnp.float32)).astype(bf16)

    if with_point:

        @pl.loop(0, tiles)
        def _(j):
            total = gp_ref[:, cols(j)]
            for d in range(1, nz):
                point_copy(d, j).wait_recv()
                total += gpr[d - 1, j].astype(jnp.float32)
            gp_ref[:, cols(j)] = total

    @pl.when(has_low)
    def _():
        to_low(0, t).wait_send()
        to_low(1, o).wait_send()
        gh_low.wait_send()

    @pl.when(has_high)
    def _():
        to_high(0, t).wait_send()
        to_high(1, o).wait_send()
        gh_high.wait_send()

    x_side.wait_send()
    d_side.wait_send()
    m_side.wait_send()
    b_side.wait_send()
    if with_point:
        d_pair.wait_send()
        d_next.wait_send()

        @pl.loop(0, tiles)
        def _(j):
            act_copy(j).wait_send()
            for d in range(1, nz):
                point_copy(d, j).wait_send()


def kernel8(tile, ahead, *refs):
    x_hbm, w_hbm, p_hbm, d_hbm, out_ref, gi_ref, gp_ref = refs[:7]
    (w, p, xpad, rim, hid, slope, act, actp, d, dt, ct, ghpad) = refs[7:19]
    (msend, mrecv, bsend, brecv, gps, gpa, gpb) = refs[19:26]
    (load, x_s, x_r, d_s, d_r, rim_s, rim_r, rimf_s, rimf_r, co_s, co_r) = refs[26:37]
    (cp_s, cp_r, cf_s, cf_r, a_s, a_r, gh_s, gh_r, m_s, m_r, b_s, b_r) = refs[37:49]
    (z_s, za_r, zb_r, cte, ae) = refs[49:54]
    (am_s, am_r, eo_s, eo_r, ef_s, ef_r, ae_s, ae_r, aef_s, aef_r) = refs[54:]

    s = lax.axis_index("seq")
    t = lax.axis_index("tensor")
    o = 1 - t
    z = s // 2
    y = lax.rem(s, 2)
    pair = s + 1 - 2 * y
    T, H = out_ref.shape
    R = DILATION_BINS
    rows = gp_ref.shape[0]
    tiles = H // tile
    chunks, wide = act.shape[0], act.shape[2]
    per = tile // wide
    bf16, f32 = jnp.bfloat16, jnp.float32
    low = s > 0
    high = s < 7
    outer = lax.rem(z + 1, 4) < 2
    inner = lax.rem(z + 1, 4) >= 2
    upper = z // 2
    far_outer = 3 - 3 * upper
    far_inner = 2 - upper
    near_inner = 1 + upper
    near_outer = 3 * upper
    early = 1 - upper
    next_one, last_one = jnp.where(outer, early, upper), jnp.where(outer, upper, early)
    beside = jnp.where(outer, near_inner, near_outer)

    def remote(src, dst, send, recv, seq, tensor):
        return pltpu.make_async_remote_copy(
            src_ref=src, dst_ref=dst, send_sem=send, recv_sem=recv,
            device_id={"seq": seq, "tensor": tensor}, device_id_type=MESH,
        )

    def cols(j):
        return pl.ds(pl.multiple_of(j * tile, tile), tile)

    barrier = pltpu.get_barrier_semaphore()

    def greet(seq, tensor):
        pl.semaphore_signal(
            barrier, inc=1, device_id={"seq": seq, "tensor": tensor}, device_id_type=MESH
        )

    greet(pair, t)

    @pl.when(z > 0)
    def _():
        greet(s - 2, t)

    @pl.when(z < 3)
    def _():
        greet(s + 2, t)

    @pl.when(jnp.logical_and(y == 0, z > 0))
    def _():
        greet(s - 1, t)

    @pl.when(jnp.logical_and(y == 1, z < 3))
    def _():
        greet(s + 1, t)

    @pl.when(y == lax.rem(z, 2))
    def _():
        greet(2 * beside + 1 - y, t)

    greet(s, o)

    own = pl.ds(pl.multiple_of(t * H, H), H)
    other = pl.ds(pl.multiple_of(o * H, H), H)
    body = pl.ds(R, T)
    x_load = pltpu.make_async_copy(x_hbm, xpad.at[t, body], load.at[0])
    d_load = pltpu.make_async_copy(d_hbm, d.at[t], load.at[1])
    w_own = [
        pltpu.make_async_copy(w_hbm.at[k, own], w.at[k, own], load.at[2 + k]) for k in range(3)
    ]
    w_other = [
        pltpu.make_async_copy(w_hbm.at[k, other], w.at[k, other], load.at[5 + k])
        for k in range(3)
    ]
    p_load = pltpu.make_async_copy(p_hbm, p, load.at[8])
    for copy in [d_load, x_load] + w_own + w_other + [p_load]:
        copy.start()

    for half in range(2):
        xpad[half, pl.ds(0, R)] = jnp.zeros((R, H), bf16)
        xpad[half, pl.ds(R + T, R)] = jnp.zeros((R, H), bf16)

    @pl.when(s == 0)
    def _():
        rim[0] = jnp.zeros((2, R, H), bf16)
        ghpad[pl.ds(0, R), :] = jnp.zeros((R, H), bf16)

    @pl.when(s == 7)
    def _():
        rim[1] = jnp.zeros((2, R, H), bf16)
        ghpad[pl.ds(R + T, R), :] = jnp.zeros((R, H), bf16)

    d_load.wait()
    dt[...] = d[t].T

    def dt_block(i, side):
        return pl.ds(pl.multiple_of((2 * i + side) * rows, rows), rows)

    for i in range(2):
        ct[2 * t + i, 0] = dt[dt_block(i, y), :]

    x_load.wait()
    for copy in w_own:
        copy.wait()

    def taps(half, rows_of, j):
        total = dot_nn(xpad[half, pl.ds(0, T)], w[0, rows_of, cols(j)])
        total += dot_nn(xpad[half, pl.ds(R, T)], w[1, rows_of, cols(j)])
        return total + dot_nn(xpad[half, pl.ds(2 * R, T)], w[2, rows_of, cols(j)])

    @pl.loop(0, tiles)
    def _(j):
        hid[:, cols(j)] = taps(t, own, j)

    met = 2 + jnp.where(z > 0, 1, 0) + jnp.where(z < 3, 1, 0) + jnp.where(y == lax.rem(z, 2), 1, 0)
    pl.semaphore_wait(barrier, met + jnp.where(jnp.where(y == 0, z > 0, z < 3), 1, 0))

    to_low = remote(
        xpad.at[t, pl.ds(R, R)], rim.at[1, t], rim_s.at[0], rim_r.at[1], s - 1, t
    )
    to_high = remote(
        xpad.at[t, pl.ds(T, R)], rim.at[0, t], rim_s.at[1], rim_r.at[0], s + 1, t
    )

    def when_low(act_on):
        pl.when(low)(act_on)

    def when_high(act_on):
        pl.when(high)(act_on)

    pl.when(jnp.logical_and(y == 0, low))(to_low.start)
    when_high(to_high.start)
    pl.when(jnp.logical_and(y == 1, low))(to_low.start)
    x_side = remote(xpad.at[t, body], xpad.at[t, body], x_s, x_r, s, o)
    x_side.start()

    def cot_pair(i):
        return remote(
            dt.at[dt_block(i, 1 - y), :], ct.at[2 * t + i, 1], cp_s.at[i], cp_r.at[i], pair, t
        )

    def cot_on(i, half):
        return remote(
            ct.at[2 * t + i, 1], ct.at[2 * half + i, 1], cf_s.at[i], cf_r.at[i], s, o
        )

    cot_own = [
        remote(ct.at[2 * t + i, 0], ct.at[2 * t + i, 0], co_s.at[i], co_r.at[i], s, o)
        for i in range(2)
    ]

    def each(copies, what):
        def run():
            for copy in copies:
                getattr(copy, what)()
        return run

    pl.when(t == early)(cot_pair(early).start)

    def cot_ahead(i, side):
        return remote(
            dt.at[dt_block(i, (y if side == 0 else 1 - y)), :], cte.at[2 * t + i, side],
            eo_s.at[i, side], eo_r.at[i, side], 2 * near_inner + (y if side == 0 else 1 - y), t,
        )

    def cot_ahead_on(i, side, half):
        return remote(
            cte.at[2 * t + i, side], cte.at[2 * half + i, side],
            ef_s.at[i, side], ef_r.at[i, side], s, o,
        )

    sends_ahead = jnp.logical_and(outer, ahead > 0)
    takes_ahead = jnp.logical_and(inner, ahead > 0)

    mine_ahead = jnp.where(t == early, 1 - early, early)
    theirs_ahead = jnp.where(o == early, 1 - early, early)

    @pl.when(sends_ahead)
    def _():
        for side in range(2):
            cot_ahead(mine_ahead, side).start()

    d_side = remote(d.at[t], d.at[t], d_s, d_r, s, o)
    d_side.start()
    each(cot_own, "start")()

    remote(xpad.at[t, body], xpad.at[o, body], x_s, x_r, s, o).wait_recv()
    for copy in w_other:
        copy.wait()

    def act_copy(c):
        return remote(act.at[c], actp.at[c], a_s.at[c], a_r.at[c], pair, t)

    edges = (pl.ds(R, T - 2 * R), pl.ds(0, R), pl.ds(T - R, R))

    def act_part(c, k):
        return remote(
            act.at[c, edges[k]], actp.at[c, edges[k]], am_s.at[c, k], am_r.at[c, k], pair, t
        )

    def act_copies(c):
        return [act_part(c, k) for k in range(3)] if c < per else [act_copy(c)]

    def activate(j, rows_of):
        value, derivative = gelu_pair(hid[rows_of, cols(j)])
        value = value.astype(bf16)
        for i in range(per):
            act[per * j + i, rows_of] = value[:, i * wide:(i + 1) * wide]
        slope[rows_of, cols(j)] = derivative

    first_sent = list(range(per))

    def middle_rows(j):
        hid[:, cols(j)] += taps(o, other, j)
        activate(j, edges[0])

    middle_rows(0)
    act_part(first_sent[0], 0).start()
    pl.when(t == early)(cot_pair(1 - early).start)
    pl.when(jnp.logical_and(t != early, inner))(cot_pair(next_one).start)

    @pl.loop(1, tiles)
    def _(j):
        middle_rows(j)

    def rim_on(k):
        return remote(rim.at[k, t], rim.at[k, t], rimf_s.at[k], rimf_r.at[k], s, o)

    def rim_land(k):
        remote(xpad.at[t, pl.ds(R, R)], rim.at[k, t], rim_s.at[0], rim_r.at[k], s, o).wait_recv()
        rim_on(k).start()

    def rim_land_on(k):
        remote(rim.at[k, t], rim.at[k, o], rimf_s.at[k], rimf_r.at[k], s, o).wait_recv()

    when_low(functools.partial(rim_land, 0))
    when_high(functools.partial(rim_land, 1))
    when_low(functools.partial(rim_land_on, 0))
    when_high(functools.partial(rim_land_on, 1))

    def edge_rows(j):
        at = cols(j)
        first = dot_nn(rim[0, 0], w[0, pl.ds(0, H), at]) + dot_nn(rim[0, 1], w[0, pl.ds(H, H), at])
        last = dot_nn(rim[1, 0], w[2, pl.ds(0, H), at]) + dot_nn(rim[1, 1], w[2, pl.ds(H, H), at])
        hid[edges[1], at] += first
        hid[edges[2], at] += last
        activate(j, edges[1])
        activate(j, edges[2])

    def act_ahead(c):
        return remote(
            act.at[c], ae.at[0, c], ae_s.at[c], ae_r.at[c], 2 * near_inner + y, t
        )

    def act_ahead_on(c):
        return remote(ae.at[0, c], ae.at[1, c], aef_s.at[c], aef_r.at[c], pair, t)

    edge_rows(0)
    act_part(first_sent[0], 1).start()
    act_part(first_sent[0], 2).start()
    for c in first_sent[1:]:
        for k in range(3):
            act_part(c, k).start()

    @pl.when(outer)
    def _():
        for c in range(ahead):
            act_ahead(c).start()

    def last_parts():
        pl.when(t != early)(cot_pair(last_one).start)

    for j in range(1, tiles):
        edge_rows(j)
        for c in range(per * j, per * j + per):
            act_copy(c).start()

    pl.when(jnp.logical_and(t != early, outer))(cot_pair(next_one).start)

    def cot_land(i):
        cot_pair(i).wait_recv()
        cot_on(i, t).start()

    def cot_land_late(i):
        @pl.when(t != early)
        def _():
            cot_land(i)

    def cot_land_late_on(i):
        @pl.when(t == early)
        def _():
            cot_on(i, o).wait_recv()

    pl.when(t == early)(functools.partial(cot_land, early))

    remote(d.at[t], d.at[o], d_s, d_r, s, o).wait_recv()
    p_load.wait()

    @pl.loop(0, tiles)
    def _(j):
        grad = dot_nn(d[0], p[pl.ds(0, H), cols(j)]) + dot_nn(d[1], p[pl.ds(H, H), cols(j)])
        ghpad[pl.ds(R, T), cols(j)] = (grad * slope[:, cols(j)]).astype(bf16)

    gh_low = remote(
        ghpad.at[pl.ds(R, R), :], ghpad.at[pl.ds(R + T, R), :], gh_s.at[0], gh_r.at[1], s - 1, t
    )
    gh_high = remote(
        ghpad.at[pl.ds(T, R), :], ghpad.at[pl.ds(0, R), :], gh_s.at[1], gh_r.at[0], s + 1, t
    )

    def gh_send():
        when_low(gh_low.start)
        when_high(gh_high.start)


    def act_tile(i):
        return jnp.concatenate([act[per * i + k] for k in range(per)], axis=1)

    def mixed(at):
        total = dot_nt(act_tile(0), p[at, pl.ds(0, tile)])
        for i in range(1, tiles):
            total += dot_nt(act_tile(i), p[at, pl.ds(i * tile, tile)])
        return total.astype(bf16)

    def back(at):
        total = dot_nt(ghpad[pl.ds(2 * R, T), :], w[0, at, :])
        total += dot_nt(ghpad[pl.ds(R, T), :], w[1, at, :])
        total += dot_nt(ghpad[pl.ds(0, T), :], w[2, at, :])
        return total.astype(bf16)

    def rows_at(half, j):
        return pl.ds(pl.multiple_of(half * H + j * tile, tile), tile)

    m_side = remote(msend, mrecv, m_s, m_r, s, o)
    b_side = remote(bsend, brecv, b_s, b_r, s, o)

    def mixed_other():
        @pl.loop(0, tiles)
        def _(j):
            msend[:, cols(j)] = mixed(rows_at(o, j))
        m_side.start()

    def mixed_own():
        m_side.wait_recv()

        @pl.loop(0, tiles)
        def _(j):
            total = xpad[t, body, cols(j)].astype(f32) + mixed(rows_at(t, j)).astype(f32)
            out_ref[:, cols(j)] = (total + mrecv[:, cols(j)].astype(f32)).astype(bf16)

    def back_other(first, last):
        @pl.loop(first, last)
        def _(j):
            bsend[:, cols(j)] = back(rows_at(o, j))

    def back_own(first, last):
        @pl.loop(first, last)
        def _(j):
            total = d[t, :, cols(j)].astype(f32) + back(rows_at(t, j)).astype(f32)
            gi_ref[:, cols(j)] = (total + brecv[:, cols(j)].astype(f32)).astype(bf16)

    def gh_land():
        def land(k):
            remote(
                ghpad.at[pl.ds(R, R), :], ghpad.at[pl.ds(k * (R + T), R), :],
                gh_s.at[0], gh_r.at[k], s, o,
            ).wait_recv()
        when_low(functools.partial(land, 0))
        when_high(functools.partial(land, 1))

    def block(zd, c):
        return dot_nn(ct[zd, 0], act[c]) + dot_nn(ct[zd, 1], actp[c])

    def block_ahead(zd, c):
        return dot_nn(cte[zd, 0], ae[0, c]) + dot_nn(cte[zd, 1], ae[1, c])

    def to_a(k, c, zt):
        return remote(gps.at[k, c], gpa.at[k, c], z_s.at[k, c], za_r.at[k, c], 2 * zt + y, t)

    def to_end(c, zt):
        return remote(gps.at[2, c], gpa.at[0, c], z_s.at[2, c], za_r.at[0, c], 2 * zt + y, t)

    def to_b(k, c, zt):
        return remote(gps.at[k, c], gpb.at[k, c], z_s.at[k, c], zb_r.at[k, c], 2 * zt + y, t)

    def act_land(c):
        for copy in act_copies(c):
            copy.wait_recv()

    def feed(k, c):
        zd = (far_outer, far_inner, near_inner)[k]
        gps[k, c] = block(zd, c).astype(bf16)
        to_a(k, c, near_inner).start()

    def ahead_land():
        for side in range(2):
            cot_ahead(mine_ahead, side).wait_recv()
            cot_ahead_on(mine_ahead, side, t).start()

    def act_ahead_land():
        for c in range(ahead):
            act_ahead(c).wait_recv()
            act_ahead_on(c).start()

    def ahead_land_on():
        for side in range(2):
            cot_ahead_on(theirs_ahead, side, o).wait_recv()
        for c in range(ahead):
            act_ahead_on(c).wait_recv()

    def middle_ahead(c):
        gps[1, c] = (block(far_inner, c) + block_ahead(far_inner, c)).astype(bf16)
        to_b(1, c, far_inner).start()

    def middle(k, c):
        part = block((far_outer, far_inner)[k], c)
        to_a(k, c, near_inner).wait_recv()
        gps[k, c] = (part + gpa[k, c].astype(f32)).astype(bf16)
        to_b(k, c, far_inner).start()

    def back_to_end(c):
        part = block(near_outer, c)
        to_b(0, c, far_inner).wait_recv()
        gps[2, c] = (part + gpb[0, c].astype(f32)).astype(bf16)
        to_end(c, near_outer).start()

    def chunk_cols(c):
        return pl.ds(pl.multiple_of(c * wide, wide), wide)

    def own_block(c):
        gp_ref[:, chunk_cols(c)] = block(z, c)

    @pl.when(t != early)
    def _():
        cot_on(early, o).wait_recv()

    @pl.when(t == early)
    def _():
        cot_land(1 - early)

    for i in range(2):
        remote(ct.at[2 * t + i, 0], ct.at[2 * o + i, 0], co_s.at[i], co_r.at[i], s, o).wait_recv()

    def far_inner_ready():
        @pl.when(t != early)
        def _():
            cot_on(1 - early, o).wait_recv()

    def back_first():
        gh_land()
        back_other(0, tiles)
        b_side.start()

    def own_blocks():
        for c in range(chunks):
            own_block(c)

    def back_last():
        b_side.wait_recv()
        back_own(0, tiles)

    rest = list(range(ahead, chunks))

    gh_send()

    @pl.when(outer)
    def _():
        last_parts()
        act_land(0)
        feed(0, 0)
        mixed_other()
        far_inner_ready()
        for c in range(1, chunks):
            act_land(c)
            feed(0, c)
            if c - 1 in rest:
                feed(1, c - 1)
            if c == 1:
                mixed_own()
        feed(1, chunks - 1)
        cot_land_late(next_one)
        cot_land_late_on(next_one)
        for c in rest:
            feed(2, c)
        cot_land_late(last_one)
        cot_land_late_on(last_one)
        own_blocks()
        back_first()
        back_last()

    @pl.when(inner)
    def _():
        mixed_other()
        far_inner_ready()
        if ahead:
            ahead_land()
        mixed_own()
        act_ahead_land()
        last_parts()
        cot_land_late(next_one)
        act_land(0)
        middle(0, 0)
        cot_land_late_on(next_one)
        for c in range(1, chunks):
            act_land(c)
            middle(0, c)
            if c > 1:
                back_to_end(c - 2)
            if c - 1 in rest:
                middle(1, c - 1)
        back_to_end(chunks - 2)
        back_first()
        back_to_end(chunks - 1)
        middle(1, chunks - 1)
        if ahead:
            ahead_land_on()
            for c in range(ahead):
                middle_ahead(c)
        cot_land_late(last_one)
        cot_land_late_on(last_one)
        own_blocks()
        for c in range(ahead):
            gp_ref[:, chunk_cols(c)] += block_ahead(z, c)
        back_last()

    for c in range(chunks):
        @pl.when(outer)
        def _():
            to_end(c, near_outer).wait_recv()
            gp_ref[:, chunk_cols(c)] += gpa[0, c].astype(f32)

        @pl.when(inner)
        def _():
            to_b(1, c, far_inner).wait_recv()
            part = gp_ref[:, chunk_cols(c)] + gpb[1, c].astype(f32)
            if c >= ahead:
                to_a(2, c, near_inner).wait_recv()
                part += gpa[2, c].astype(f32)
            gp_ref[:, chunk_cols(c)] = part

    when_low(to_low.wait_send)
    when_high(to_high.wait_send)
    when_low(rim_on(0).wait_send)
    when_high(rim_on(1).wait_send)
    when_low(gh_low.wait_send)
    when_high(gh_high.wait_send)
    for copy in [x_side, d_side, m_side, b_side] + cot_own:
        copy.wait_send()
    for i in range(2):
        cot_pair(i).wait_send()
        cot_on(i, t).wait_send()
    for c in range(chunks):
        for copy in act_copies(c):
            copy.wait_send()
        if c >= ahead:
            for k in range(3):
                to_a(k, c, near_inner).wait_send()

    @pl.when(sends_ahead)
    def _():
        for side in range(2):
            cot_ahead(mine_ahead, side).wait_send()
        for c in range(ahead):
            act_ahead(c).wait_send()
            to_a(0, c, near_inner).wait_send()

    @pl.when(takes_ahead)
    def _():
        for side in range(2):
            cot_ahead_on(mine_ahead, side, t).wait_send()
        for c in range(ahead):
            act_ahead_on(c).wait_send()
            for k in range(3):
                to_a(k, c, near_inner).wait_send()


def writer(out_ref, gi_ref, gp_ref, out_hbm, gi_hbm, gp_hbm, sem):
    copies = [
        pltpu.make_async_copy(src, dst, sem.at[i])
        for i, (src, dst) in enumerate(
            ((gp_ref, gp_hbm), (out_ref, out_hbm), (gi_ref, gi_hbm))
        )
    ]
    for copy in copies:
        copy.start()
    for copy in copies:
        copy.wait()


def local8(inputs, w_dilated, w_point, cotangent):
    T, H = inputs.shape
    C = w_point.shape[0]
    R = DILATION_BINS
    tile, wide, ahead = 256, 128, 0
    tiles, chunks = H // tile, H // wide
    rows = C // 8
    bf16, f32 = jnp.bfloat16, jnp.float32
    dma = pltpu.SemaphoreType.DMA
    vmem = pl.BlockSpec(memory_space=pltpu.VMEM)
    hbm = pl.BlockSpec(memory_space=pltpu.HBM)
    shapes = [
        ((3, C, H), bf16), ((C, H), bf16), ((2, T + 2 * R, H), bf16), ((2, 2, R, H), bf16),
        ((T, H), f32), ((T, H), f32), ((chunks, T, wide), bf16), ((chunks, T, wide), bf16),
        ((2, T, H), bf16), ((H, T), bf16), ((4, 2, rows, T), bf16), ((T + 2 * R, H), bf16),
        ((T, H), bf16), ((T, H), bf16), ((T, H), bf16), ((T, H), bf16),
        ((3, chunks, rows, wide), bf16), ((3, chunks, rows, wide), bf16),
        ((2, chunks, rows, wide), bf16),
    ]
    one = dma(())
    two = dma((2,))
    sems = [
        dma((9,)), one, one, one, one, two, two, two, two, two, two,
        two, two, two, two, dma((chunks,)), dma((chunks,)), two, two, one, one, one, one,
        dma((3, chunks)), dma((3, chunks)), dma((2, chunks)),
    ]
    held = max(ahead, 1)
    late = [
        ((4, 2, rows, T), bf16), ((2, held, T, wide), bf16),
    ]
    late_sems = [
        dma((tile // wide, 3)), dma((tile // wide, 3)), dma((2, 2)), dma((2, 2)), dma((2, 2)),
        dma((2, 2)), dma((held,)), dma((held,)), dma((held,)), dma((held,)),
    ]
    outs = [
        jax.ShapeDtypeStruct((T, H), bf16),
        jax.ShapeDtypeStruct((T, H), bf16),
        jax.ShapeDtypeStruct((rows, H), f32),
    ]
    results = pl.pallas_call(
        functools.partial(kernel8, tile, ahead),
        out_shape=[pltpu.VMEM(out.shape, out.dtype) for out in outs],
        in_specs=[hbm] * 4,
        out_specs=[vmem] * 3,
        scratch_shapes=[pltpu.VMEM(*shape) for shape in shapes] + sems
        + [pltpu.VMEM(*shape) for shape in late] + late_sems,
        compiler_params=pltpu.CompilerParams(
            collective_id=0, has_side_effects=True, vmem_limit_bytes=60 * 1024 * 1024
        ),
    )(inputs, jnp.transpose(w_dilated, (1, 0, 2)), w_point, cotangent)
    return tuple(
        pl.pallas_call(
            writer,
            out_shape=outs,
            in_specs=[vmem] * 3,
            out_specs=[hbm] * 3,
            scratch_shapes=[dma((3,))],
            compiler_params=pltpu.CompilerParams(vmem_limit_bytes=1024 * 1024),
        )(*results)
    )


def local(n, inputs, w_dilated, w_point, cotangent):
    if n == 8 and inputs.shape[0] == 256:
        return local8(inputs, w_dilated, w_point, cotangent)
    T, H = inputs.shape
    C = w_point.shape[0]
    R = DILATION_BINS
    tile = 256
    tiles = H // tile
    rows = C // n
    bf16, f32 = jnp.bfloat16, jnp.float32
    with_point = rows % 16 == 0 and n % 2 == 0
    nz = n // 2
    vmem = pl.BlockSpec(memory_space=pltpu.VMEM)
    hbm = pl.BlockSpec(memory_space=pl.ANY)
    plane = jax.ShapeDtypeStruct((T, H), bf16)
    act_shape = (tiles, T, tile)
    outs = [plane, plane]
    scratch = []
    if with_point:
        outs += [jax.ShapeDtypeStruct((rows, H), f32)]
        scratch += [pltpu.VMEM(act_shape, bf16), pltpu.VMEM((T, C), bf16)]
    else:
        outs += [jax.ShapeDtypeStruct(act_shape, bf16), jax.ShapeDtypeStruct((T, C), bf16)]
    dma = pltpu.SemaphoreType.DMA
    scratch += [
        pltpu.VMEM((3, C, H), bf16),
        pltpu.VMEM((C, H), bf16),
        pltpu.VMEM((T + 2 * R, C), bf16),
        pltpu.VMEM((T, H), f32),
        pltpu.VMEM((T + 2 * R, H), bf16),
        pltpu.VMEM((T, H), bf16),
        pltpu.VMEM((T, H), bf16),
        pltpu.VMEM((T, H), bf16),
        pltpu.VMEM((T, H), bf16),
        dma((4,)), dma((6,)), dma((6,)), dma((4,)), dma((4,)), dma((2,)), dma((2,)),
    ]
    if with_point:
        scratch += [
            pltpu.VMEM(act_shape, bf16),
            pltpu.VMEM((T, H), bf16),
            pltpu.VMEM((T, H), bf16),
            pltpu.VMEM((C, 2 * T), bf16),
            pltpu.VMEM((nz - 1, tiles, rows, tile), bf16),
            pltpu.VMEM((nz - 1, tiles, rows, tile), bf16),
            dma((tiles,)), dma((tiles,)), dma((nz - 1, tiles)), dma((nz - 1, tiles)),
        ]
    results = pl.pallas_call(
        functools.partial(kernel, n, tile, with_point),
        out_shape=outs,
        in_specs=[vmem, hbm, hbm, vmem],
        out_specs=[vmem] * len(outs),
        scratch_shapes=scratch,
        compiler_params=pltpu.CompilerParams(
            collective_id=0, has_side_effects=True, vmem_limit_bytes=48 * 1024 * 1024
        ),
    )(inputs, jnp.transpose(w_dilated, (1, 0, 2)), w_point, cotangent)
    if with_point:
        return tuple(results)
    output, grad_inputs, act, full_grad = results
    activation = jnp.transpose(act, (1, 0, 2)).reshape(T, H)
    grad_point = lax.psum_scatter(
        jnp.einsum("to,tc->oc", full_grad, activation, preferred_element_type=f32),
        "seq",
        scatter_dimension=0,
        tiled=True,
    )
    return (output, grad_inputs, grad_point)


def solution(mesh):
    placed = (
        P(("groups", "seq"), "tensor"),
        P(None, None, "tensor"),
        P(None, "tensor"),
        P(("groups", "seq"), "tensor"),
    )
    return jax.shard_map(
        functools.partial(local, mesh.shape["seq"]),
        mesh=mesh,
        in_specs=placed,
        out_specs=(
            P(("groups", "seq"), "tensor"),
            P(("groups", "seq"), "tensor"),
            P(("groups", "seq"), "tensor"),
        ),
        check_vma=False,
    )
```

```python
import functools
import math

import jax
import jax.numpy as jnp
from jax import lax
from jax.experimental import pallas as pl
from jax.experimental.pallas import tpu as pltpu
from jax.sharding import PartitionSpec as P

DILATION_BINS = 32
MESH = pl.DeviceIdType.MESH

gelu_cubic = 0.044715
gelu_scale = math.sqrt(2.0 / math.pi)


def gelu_pair(values):
    square = values * values
    tangent = jnp.tanh(gelu_scale * (values + gelu_cubic * square * values))
    half = 0.5 * (1.0 + tangent)
    slope = half + 0.5 * values * (1.0 - tangent * tangent) * gelu_scale * (
        1.0 + 3.0 * gelu_cubic * square
    )
    return values * half, slope


def dot_nn(a, b):
    return jnp.dot(a, b, preferred_element_type=jnp.float32)


def dot_nt(a, b):
    return lax.dot_general(a, b, (((1,), (1,)), ((), ())), preferred_element_type=jnp.float32)


def kernel(n, tile, with_point, *refs):
    x_ref, w_hbm, p_hbm, d_ref = refs[:4]
    if with_point:
        out_ref, gi_ref, gp_ref = refs[4:7]
        act, dfull = refs[7:9]
        rest = refs[9:]
    else:
        out_ref, gi_ref, act, dfull = refs[4:8]
        rest = refs[8:]
    (w, p, xfull, slope, ghpad, msend, mrecv, bsend, brecv) = rest[:9]
    (lsem, ssem, rsem, xs_sem, xr_sem, gs_sem, gr_sem) = rest[9:16]
    if with_point:
        (actp, dp, dps, cot_t, gps, gpr, as_sem, ar_sem, ps_sem, pr_sem) = rest[16:]

    s = lax.axis_index("seq")
    t = lax.axis_index("tensor")
    o = 1 - t
    T, H = x_ref.shape
    C = 2 * H
    R = DILATION_BINS
    tiles = H // tile
    bf16 = jnp.bfloat16
    has_low = s > 0
    has_high = s < n - 1
    mine = pl.ds(pl.multiple_of(t * H, H), H)
    other = pl.ds(pl.multiple_of(o * H, H), H)
    nz = n // 2
    z = s // 2
    y = lax.rem(s, 2)
    pair = s + 1 - 2 * y

    def remote(src, dst, send, recv, seq, tensor):
        return pltpu.make_async_remote_copy(
            src_ref=src,
            dst_ref=dst,
            send_sem=send,
            recv_sem=recv,
            device_id={"seq": seq, "tensor": tensor},
            device_id_type=MESH,
        )

    def cols(j):
        return pl.ds(pl.multiple_of(j * tile, tile), tile)

    w_loads = [pltpu.make_async_copy(w_hbm.at[k], w.at[k], lsem.at[k]) for k in range(3)]
    p_load = pltpu.make_async_copy(p_hbm, p, lsem.at[3])
    for load in w_loads:
        load.start()
    p_load.start()

    barrier = pltpu.get_barrier_semaphore()

    def greet(seq, tensor):
        pl.semaphore_signal(
            barrier, inc=1, device_id={"seq": seq, "tensor": tensor}, device_id_type=MESH
        )

    greet(s, o)

    @pl.when(has_low)
    def _():
        greet(s - 1, t)
        greet(s - 1, o)

    @pl.when(has_high)
    def _():
        greet(s + 1, t)
        greet(s + 1, o)

    if with_point:
        for d in range(1, nz):
            greet(lax.rem(z + d, nz) * 2 + y, t)
    xfull[pl.ds(R, T), mine] = x_ref[...]
    dfull[:, mine] = d_ref[...]
    sides = lax.div(s + n - 1, n) + lax.div(2 * n - 2 - s, n)
    pl.semaphore_wait(barrier, 1 + (nz - 1 if with_point else 0) + 2 * sides)

    def to_low(slot, tensor):
        return remote(
            x_ref.at[pl.ds(0, R), :], xfull.at[pl.ds(R + T, R), mine],
            xs_sem.at[slot], xr_sem.at[2 + t], s - 1, tensor,
        )

    def to_high(slot, tensor):
        return remote(
            x_ref.at[pl.ds(T - R, R), :], xfull.at[pl.ds(0, R), mine],
            xs_sem.at[2 + slot], xr_sem.at[t], s + 1, tensor,
        )

    @pl.when(has_low)
    def _():
        to_low(0, t).start()
        to_low(1, o).start()

    @pl.when(has_high)
    def _():
        to_high(0, t).start()
        to_high(1, o).start()

    x_side = remote(x_ref, xfull.at[pl.ds(R, T), mine], ssem.at[0], rsem.at[0], s, o)
    x_side.start()
    d_side = remote(d_ref, dfull.at[:, mine], ssem.at[1], rsem.at[1], s, o)
    d_side.start()
    if with_point:
        d_pair = remote(d_ref, dp, ssem.at[2], rsem.at[2], pair, t)
        d_pair.start()
        d_next = remote(dp, dps, ssem.at[3], rsem.at[3], s, o)
        cot_t[mine, pl.ds(0, T)] = d_ref[...].T

    @pl.when(s == 0)
    def _():
        xfull[pl.ds(0, R), :] = jnp.zeros((R, C), bf16)
        ghpad[pl.ds(0, R), :] = jnp.zeros((R, H), bf16)

    @pl.when(s == n - 1)
    def _():
        xfull[pl.ds(R + T, R), :] = jnp.zeros((R, C), bf16)
        ghpad[pl.ds(R + T, R), :] = jnp.zeros((R, H), bf16)

    remote(x_ref, xfull.at[pl.ds(R, T), other], ssem.at[0], rsem.at[0], s, o).wait_recv()

    @pl.when(has_low)
    def _():
        for half in range(2):
            remote(
                x_ref.at[pl.ds(0, R), :], xfull.at[pl.ds(0, R), pl.ds(half * H, H)],
                xs_sem.at[0], xr_sem.at[half], s - 1, t,
            ).wait_recv()

    @pl.when(has_high)
    def _():
        for half in range(2):
            remote(
                x_ref.at[pl.ds(0, R), :], xfull.at[pl.ds(R + T, R), pl.ds(half * H, H)],
                xs_sem.at[0], xr_sem.at[2 + half], s + 1, t,
            ).wait_recv()

    for load in w_loads:
        load.wait()

    def act_copy(j):
        return remote(
            act.at[j], actp.at[j], as_sem.at[j], ar_sem.at[j], pair, t
        )

    @pl.loop(0, tiles)
    def _(j):
        hidden = dot_nn(xfull[pl.ds(0, T), :], w[0, :, cols(j)])
        hidden += dot_nn(xfull[pl.ds(R, T), :], w[1, :, cols(j)])
        hidden += dot_nn(xfull[pl.ds(2 * R, T), :], w[2, :, cols(j)])
        value, derivative = gelu_pair(hidden)
        act[j] = value.astype(bf16)
        slope[:, cols(j)] = derivative
        if with_point:
            act_copy(j).start()

    if with_point:
        remote(d_ref, dp, ssem.at[2], rsem.at[2], pair, t).wait_recv()
        d_next.start()
        cot_t[mine, pl.ds(T, T)] = dp[...].T
    remote(d_ref, dfull.at[:, other], ssem.at[1], rsem.at[1], s, o).wait_recv()
    p_load.wait()
    if with_point:
        cot_t[other, pl.ds(0, T)] = dfull[:, other].T

    @pl.loop(0, tiles)
    def _(j):
        grad = dot_nn(dfull[...], p[:, cols(j)]) * slope[:, cols(j)]
        ghpad[pl.ds(R, T), cols(j)] = grad.astype(bf16)

    gh_low = remote(
        ghpad.at[pl.ds(R, R), :], ghpad.at[pl.ds(R + T, R), :],
        gs_sem.at[0], gr_sem.at[1], s - 1, t,
    )
    gh_high = remote(
        ghpad.at[pl.ds(T, R), :], ghpad.at[pl.ds(0, R), :],
        gs_sem.at[1], gr_sem.at[0], s + 1, t,
    )

    @pl.when(has_low)
    def _():
        gh_low.start()

    @pl.when(has_high)
    def _():
        gh_high.start()

    def point_copy(d, j):
        return remote(
            gps.at[d - 1, j], gpr.at[d - 1, j], ps_sem.at[d - 1, j], pr_sem.at[d - 1, j],
            lax.rem(z + d, nz) * 2 + y, t,
        )

    if with_point:
        rows = gp_ref.shape[0]
        remote(dp, dps, ssem.at[3], rsem.at[3], s, o).wait_recv()
        cot_t[other, pl.ds(T, T)] = dps[...].T

        @pl.loop(0, tiles)
        def _(j):
            act_copy(j).wait_recv()

            def block(d):
                owner = lax.rem(z + d, nz) * 2 + y
                at = pl.ds(pl.multiple_of(owner * rows, rows), rows)
                return dot_nn(cot_t[at, pl.ds(0, T)], act[j]) + dot_nn(
                    cot_t[at, pl.ds(T, T)], actp[j]
                )

            for d in range(1, nz):
                gps[d - 1, j] = block(d).astype(bf16)
                point_copy(d, j).start()
            gp_ref[:, cols(j)] = block(0)

    def mixed(at):
        total = dot_nt(act[0], p[at, pl.ds(0, tile)])
        for i in range(1, tiles):
            total += dot_nt(act[i], p[at, pl.ds(i * tile, tile)])
        return total.astype(bf16)

    @pl.loop(0, tiles)
    def _(j):
        msend[:, cols(j)] = mixed(pl.ds(pl.multiple_of(o * H + j * tile, tile), tile))

    m_side = remote(msend, mrecv, ssem.at[4], rsem.at[4], s, o)
    m_side.start()

    @pl.when(has_low)
    def _():
        remote(
            ghpad.at[pl.ds(R, R), :], ghpad.at[pl.ds(0, R), :],
            gs_sem.at[0], gr_sem.at[0], s - 1, t,
        ).wait_recv()

    @pl.when(has_high)
    def _():
        remote(
            ghpad.at[pl.ds(R, R), :], ghpad.at[pl.ds(R + T, R), :],
            gs_sem.at[0], gr_sem.at[1], s + 1, t,
        ).wait_recv()

    def back(at):
        total = dot_nt(ghpad[pl.ds(2 * R, T), :], w[0, at, :])
        total += dot_nt(ghpad[pl.ds(R, T), :], w[1, at, :])
        total += dot_nt(ghpad[pl.ds(0, T), :], w[2, at, :])
        return total.astype(bf16)

    @pl.loop(0, tiles)
    def _(j):
        bsend[:, cols(j)] = back(pl.ds(pl.multiple_of(o * H + j * tile, tile), tile))

    b_side = remote(bsend, brecv, ssem.at[5], rsem.at[5], s, o)
    b_side.start()
    m_side.wait_recv()

    @pl.loop(0, tiles)
    def _(j):
        own = mixed(pl.ds(pl.multiple_of(t * H + j * tile, tile), tile))
        total = x_ref[:, cols(j)].astype(jnp.float32) + own.astype(jnp.float32)
        out_ref[:, cols(j)] = (total + mrecv[:, cols(j)].astype(jnp.float32)).astype(bf16)

    b_side.wait_recv()

    @pl.loop(0, tiles)
    def _(j):
        own = back(pl.ds(pl.multiple_of(t * H + j * tile, tile), tile))
        total = d_ref[:, cols(j)].astype(jnp.float32) + own.astype(jnp.float32)
        gi_ref[:, cols(j)] = (total + brecv[:, cols(j)].astype(jnp.float32)).astype(bf16)

    if with_point:

        @pl.loop(0, tiles)
        def _(j):
            total = gp_ref[:, cols(j)]
            for d in range(1, nz):
                point_copy(d, j).wait_recv()
                total += gpr[d - 1, j].astype(jnp.float32)
            gp_ref[:, cols(j)] = total

    @pl.when(has_low)
    def _():
        to_low(0, t).wait_send()
        to_low(1, o).wait_send()
        gh_low.wait_send()

    @pl.when(has_high)
    def _():
        to_high(0, t).wait_send()
        to_high(1, o).wait_send()
        gh_high.wait_send()

    x_side.wait_send()
    d_side.wait_send()
    m_side.wait_send()
    b_side.wait_send()
    if with_point:
        d_pair.wait_send()
        d_next.wait_send()

        @pl.loop(0, tiles)
        def _(j):
            act_copy(j).wait_send()
            for d in range(1, nz):
                point_copy(d, j).wait_send()


def kernel8(tile, ahead, *refs):
    x_hbm, w_hbm, p_hbm, d_hbm, out_ref, gi_ref, gp_ref = refs[:7]
    (w, p, xpad, rim, hid, slope, act, actp, d, dt, ct, ghpad) = refs[7:19]
    (msend, mrecv, bsend, brecv, gps, gpa, gpb) = refs[19:26]
    (load, x_s, x_r, d_s, d_r, rim_s, rim_r, rimf_s, rimf_r, co_s, co_r) = refs[26:37]
    (cp_s, cp_r, cf_s, cf_r, a_s, a_r, gh_s, gh_r, m_s, m_r, b_s, b_r) = refs[37:49]
    (z_s, za_r, zb_r, cte, ae) = refs[49:54]
    (am_s, am_r, eo_s, eo_r, ef_s, ef_r, ae_s, ae_r, aef_s, aef_r) = refs[54:]

    s = lax.axis_index("seq")
    t = lax.axis_index("tensor")
    o = 1 - t
    z = s // 2
    y = lax.rem(s, 2)
    pair = s + 1 - 2 * y
    T, H = out_ref.shape
    R = DILATION_BINS
    rows = gp_ref.shape[0]
    tiles = H // tile
    chunks, wide = act.shape[0], act.shape[2]
    per = tile // wide
    bf16, f32 = jnp.bfloat16, jnp.float32
    low = s > 0
    high = s < 7
    outer = lax.rem(z + 1, 4) < 2
    inner = lax.rem(z + 1, 4) >= 2
    upper = z // 2
    far_outer = 3 - 3 * upper
    far_inner = 2 - upper
    near_inner = 1 + upper
    near_outer = 3 * upper
    early = 1 - upper
    next_one, last_one = jnp.where(outer, early, upper), jnp.where(outer, upper, early)
    beside = jnp.where(outer, near_inner, near_outer)

    def remote(src, dst, send, recv, seq, tensor):
        return pltpu.make_async_remote_copy(
            src_ref=src, dst_ref=dst, send_sem=send, recv_sem=recv,
            device_id={"seq": seq, "tensor": tensor}, device_id_type=MESH,
        )

    def cols(j):
        return pl.ds(pl.multiple_of(j * tile, tile), tile)

    barrier = pltpu.get_barrier_semaphore()

    def greet(seq, tensor):
        pl.semaphore_signal(
            barrier, inc=1, device_id={"seq": seq, "tensor": tensor}, device_id_type=MESH
        )

    greet(pair, t)

    @pl.when(z > 0)
    def _():
        greet(s - 2, t)

    @pl.when(z < 3)
    def _():
        greet(s + 2, t)

    @pl.when(jnp.logical_and(y == 0, z > 0))
    def _():
        greet(s - 1, t)

    @pl.when(jnp.logical_and(y == 1, z < 3))
    def _():
        greet(s + 1, t)

    crossed = jnp.logical_and(y == lax.rem(z, 2), ahead > 0)

    @pl.when(crossed)
    def _():
        greet(2 * beside + 1 - y, t)

    greet(s, o)

    own = pl.ds(pl.multiple_of(t * H, H), H)
    other = pl.ds(pl.multiple_of(o * H, H), H)
    body = pl.ds(R, T)
    x_load = pltpu.make_async_copy(x_hbm, xpad.at[t, body], load.at[0])
    d_load = pltpu.make_async_copy(d_hbm, d.at[t], load.at[1])
    w_own = [
        pltpu.make_async_copy(w_hbm.at[k, own], w.at[k, own], load.at[2 + k]) for k in range(3)
    ]
    w_other = [
        pltpu.make_async_copy(w_hbm.at[k, other], w.at[k, other], load.at[5 + k])
        for k in range(3)
    ]
    p_load = pltpu.make_async_copy(p_hbm, p, load.at[8])
    for copy in [d_load, x_load] + w_own + w_other + [p_load]:
        copy.start()

    for half in range(2):
        xpad[half, pl.ds(0, R)] = jnp.zeros((R, H), bf16)
        xpad[half, pl.ds(R + T, R)] = jnp.zeros((R, H), bf16)

    @pl.when(s == 0)
    def _():
        rim[0] = jnp.zeros((2, R, H), bf16)
        ghpad[pl.ds(0, R), :] = jnp.zeros((R, H), bf16)

    @pl.when(s == 7)
    def _():
        rim[1] = jnp.zeros((2, R, H), bf16)
        ghpad[pl.ds(R + T, R), :] = jnp.zeros((R, H), bf16)

    d_load.wait()
    dt[...] = d[t].T

    def dt_block(i, side):
        return pl.ds(pl.multiple_of((2 * i + side) * rows, rows), rows)

    for i in range(2):
        ct[2 * t + i, 0] = dt[dt_block(i, y), :]

    x_load.wait()
    for copy in w_own:
        copy.wait()

    def taps(half, rows_of, j):
        total = dot_nn(xpad[half, pl.ds(0, T)], w[0, rows_of, cols(j)])
        total += dot_nn(xpad[half, pl.ds(R, T)], w[1, rows_of, cols(j)])
        return total + dot_nn(xpad[half, pl.ds(2 * R, T)], w[2, rows_of, cols(j)])

    @pl.loop(0, tiles)
    def _(j):
        hid[:, cols(j)] = taps(t, own, j)

    met = 2 + jnp.where(z > 0, 1, 0) + jnp.where(z < 3, 1, 0) + jnp.where(crossed, 1, 0)
    pl.semaphore_wait(barrier, met + jnp.where(jnp.where(y == 0, z > 0, z < 3), 1, 0))

    to_low = remote(
        xpad.at[t, pl.ds(R, R)], rim.at[1, t], rim_s.at[0], rim_r.at[1], s - 1, t
    )
    to_high = remote(
        xpad.at[t, pl.ds(T, R)], rim.at[0, t], rim_s.at[1], rim_r.at[0], s + 1, t
    )

    def when_low(act_on):
        pl.when(low)(act_on)

    def when_high(act_on):
        pl.when(high)(act_on)

    pl.when(jnp.logical_and(y == 0, low))(to_low.start)
    when_high(to_high.start)
    pl.when(jnp.logical_and(y == 1, low))(to_low.start)
    x_side = remote(xpad.at[t, body], xpad.at[t, body], x_s, x_r, s, o)
    x_side.start()

    def cot_pair(i):
        return remote(
            dt.at[dt_block(i, 1 - y), :], ct.at[2 * t + i, 1], cp_s.at[i], cp_r.at[i], pair, t
        )

    def cot_on(i, half):
        return remote(
            ct.at[2 * t + i, 1], ct.at[2 * half + i, 1], cf_s.at[i], cf_r.at[i], s, o
        )

    cot_own = [
        remote(ct.at[2 * t + i, 0], ct.at[2 * t + i, 0], co_s.at[i], co_r.at[i], s, o)
        for i in range(2)
    ]

    def each(copies, what):
        def run():
            for copy in copies:
                getattr(copy, what)()
        return run

    pl.when(t == early)(cot_pair(early).start)

    def cot_ahead(i, side):
        return remote(
            dt.at[dt_block(i, (y if side == 0 else 1 - y)), :], cte.at[2 * t + i, side],
            eo_s.at[i, side], eo_r.at[i, side], 2 * near_inner + (y if side == 0 else 1 - y), t,
        )

    def cot_ahead_on(i, side, half):
        return remote(
            cte.at[2 * t + i, side], cte.at[2 * half + i, side],
            ef_s.at[i, side], ef_r.at[i, side], s, o,
        )

    sends_ahead = jnp.logical_and(outer, ahead > 0)
    takes_ahead = jnp.logical_and(inner, ahead > 0)

    mine_ahead = jnp.where(t == early, 1 - early, early)
    theirs_ahead = jnp.where(o == early, 1 - early, early)

    @pl.when(sends_ahead)
    def _():
        for side in range(2):
            cot_ahead(mine_ahead, side).start()

    d_side = remote(d.at[t], d.at[t], d_s, d_r, s, o)
    d_side.start()
    each(cot_own, "start")()

    remote(xpad.at[t, body], xpad.at[o, body], x_s, x_r, s, o).wait_recv()
    for copy in w_other:
        copy.wait()

    def act_copy(c):
        return remote(act.at[c], actp.at[c], a_s.at[c], a_r.at[c], pair, t)

    edges = (pl.ds(R, T - 2 * R), pl.ds(0, R), pl.ds(T - R, R))

    def act_part(c, k):
        return remote(
            act.at[c, edges[k]], actp.at[c, edges[k]], am_s.at[c, k], am_r.at[c, k], pair, t
        )

    def act_copies(c):
        return [act_part(c, k) for k in range(3)] if c < per else [act_copy(c)]

    def activate(j, rows_of):
        value, derivative = gelu_pair(hid[rows_of, cols(j)])
        value = value.astype(bf16)
        for i in range(per):
            act[per * j + i, rows_of] = value[:, i * wide:(i + 1) * wide]
        slope[rows_of, cols(j)] = derivative

    first_sent = list(range(per))

    def middle_rows(j):
        hid[:, cols(j)] += taps(o, other, j)
        activate(j, edges[0])

    middle_rows(0)
    act_part(first_sent[0], 0).start()
    pl.when(t == early)(cot_pair(1 - early).start)
    pl.when(jnp.logical_and(t != early, inner))(cot_pair(next_one).start)

    @pl.loop(1, tiles)
    def _(j):
        middle_rows(j)

    def rim_on(k):
        return remote(rim.at[k, t], rim.at[k, t], rimf_s.at[k], rimf_r.at[k], s, o)

    def rim_land(k):
        remote(xpad.at[t, pl.ds(R, R)], rim.at[k, t], rim_s.at[0], rim_r.at[k], s, o).wait_recv()
        rim_on(k).start()

    def rim_land_on(k):
        remote(rim.at[k, t], rim.at[k, o], rimf_s.at[k], rimf_r.at[k], s, o).wait_recv()

    when_low(functools.partial(rim_land, 0))
    when_high(functools.partial(rim_land, 1))
    def rim_half(half, rows_of, j):
        at = cols(j)
        hid[edges[1], at] += dot_nn(rim[0, half], w[0, rows_of, at])
        hid[edges[2], at] += dot_nn(rim[1, half], w[2, rows_of, at])

    @pl.loop(0, tiles)
    def _(j):
        rim_half(t, own, j)

    when_low(functools.partial(rim_land_on, 0))
    when_high(functools.partial(rim_land_on, 1))

    def edge_rows(j):
        rim_half(o, other, j)
        activate(j, edges[1])
        activate(j, edges[2])

    def act_ahead(c):
        return remote(
            act.at[c], ae.at[0, c], ae_s.at[c], ae_r.at[c], 2 * near_inner + y, t
        )

    def act_ahead_on(c):
        return remote(ae.at[0, c], ae.at[1, c], aef_s.at[c], aef_r.at[c], pair, t)

    edge_rows(0)
    act_part(first_sent[0], 1).start()
    act_part(first_sent[0], 2).start()
    for c in first_sent[1:]:
        for k in range(3):
            act_part(c, k).start()

    @pl.when(outer)
    def _():
        for c in range(ahead):
            act_ahead(c).start()

    def last_parts():
        pl.when(t != early)(cot_pair(last_one).start)

    for j in range(1, tiles):
        edge_rows(j)
        for c in range(per * j, per * j + per):
            act_copy(c).start()

    pl.when(jnp.logical_and(t != early, outer))(cot_pair(next_one).start)

    def cot_land(i):
        cot_pair(i).wait_recv()
        cot_on(i, t).start()

    def cot_land_late(i):
        @pl.when(t != early)
        def _():
            cot_land(i)

    def cot_land_late_on(i):
        @pl.when(t == early)
        def _():
            cot_on(i, o).wait_recv()

    pl.when(t == early)(functools.partial(cot_land, early))

    remote(d.at[t], d.at[o], d_s, d_r, s, o).wait_recv()
    p_load.wait()

    @pl.loop(0, tiles)
    def _(j):
        grad = dot_nn(d[0], p[pl.ds(0, H), cols(j)]) + dot_nn(d[1], p[pl.ds(H, H), cols(j)])
        ghpad[pl.ds(R, T), cols(j)] = (grad * slope[:, cols(j)]).astype(bf16)

    gh_low = remote(
        ghpad.at[pl.ds(R, R), :], ghpad.at[pl.ds(R + T, R), :], gh_s.at[0], gh_r.at[1], s - 1, t
    )
    gh_high = remote(
        ghpad.at[pl.ds(T, R), :], ghpad.at[pl.ds(0, R), :], gh_s.at[1], gh_r.at[0], s + 1, t
    )

    def gh_send():
        when_low(gh_low.start)
        when_high(gh_high.start)


    def act_tile(i):
        return jnp.concatenate([act[per * i + k] for k in range(per)], axis=1)

    def mixed(at):
        total = dot_nt(act_tile(0), p[at, pl.ds(0, tile)])
        for i in range(1, tiles):
            total += dot_nt(act_tile(i), p[at, pl.ds(i * tile, tile)])
        return total.astype(bf16)

    def back(at):
        total = dot_nt(ghpad[pl.ds(2 * R, T), :], w[0, at, :])
        total += dot_nt(ghpad[pl.ds(R, T), :], w[1, at, :])
        total += dot_nt(ghpad[pl.ds(0, T), :], w[2, at, :])
        return total.astype(bf16)

    def rows_at(half, j):
        return pl.ds(pl.multiple_of(half * H + j * tile, tile), tile)

    m_side = remote(msend, mrecv, m_s, m_r, s, o)
    b_side = remote(bsend, brecv, b_s, b_r, s, o)

    def mixed_other():
        @pl.loop(0, tiles)
        def _(j):
            msend[:, cols(j)] = mixed(rows_at(o, j))
        m_side.start()

    def mixed_own():
        m_side.wait_recv()

        @pl.loop(0, tiles)
        def _(j):
            total = xpad[t, body, cols(j)].astype(f32) + mixed(rows_at(t, j)).astype(f32)
            out_ref[:, cols(j)] = (total + mrecv[:, cols(j)].astype(f32)).astype(bf16)

    def back_other(first, last):
        @pl.loop(first, last)
        def _(j):
            bsend[:, cols(j)] = back(rows_at(o, j))

    def back_own(first, last):
        @pl.loop(first, last)
        def _(j):
            total = d[t, :, cols(j)].astype(f32) + back(rows_at(t, j)).astype(f32)
            gi_ref[:, cols(j)] = (total + brecv[:, cols(j)].astype(f32)).astype(bf16)

    def gh_land():
        def land(k):
            remote(
                ghpad.at[pl.ds(R, R), :], ghpad.at[pl.ds(k * (R + T), R), :],
                gh_s.at[0], gh_r.at[k], s, o,
            ).wait_recv()
        when_low(functools.partial(land, 0))
        when_high(functools.partial(land, 1))

    def block(zd, c):
        return dot_nn(ct[zd, 0], act[c]) + dot_nn(ct[zd, 1], actp[c])

    def block_ahead(zd, c):
        return dot_nn(cte[zd, 0], ae[0, c]) + dot_nn(cte[zd, 1], ae[1, c])

    def to_a(k, c, zt):
        return remote(gps.at[k, c], gpa.at[k, c], z_s.at[k, c], za_r.at[k, c], 2 * zt + y, t)

    def to_end(c, zt):
        return remote(gps.at[2, c], gpa.at[0, c], z_s.at[2, c], za_r.at[0, c], 2 * zt + y, t)

    def to_b(k, c, zt):
        return remote(gps.at[k, c], gpb.at[k, c], z_s.at[k, c], zb_r.at[k, c], 2 * zt + y, t)

    def act_land(c):
        for copy in act_copies(c):
            copy.wait_recv()

    def feed(k, c):
        zd = (far_outer, far_inner, near_inner)[k]
        gps[k, c] = block(zd, c).astype(bf16)
        to_a(k, c, near_inner).start()

    def ahead_land():
        for side in range(2):
            cot_ahead(mine_ahead, side).wait_recv()
            cot_ahead_on(mine_ahead, side, t).start()

    def act_ahead_land():
        for c in range(ahead):
            act_ahead(c).wait_recv()
            act_ahead_on(c).start()

    def ahead_land_on():
        for side in range(2):
            cot_ahead_on(theirs_ahead, side, o).wait_recv()
        for c in range(ahead):
            act_ahead_on(c).wait_recv()

    def middle_ahead(c):
        gps[1, c] = (block(far_inner, c) + block_ahead(far_inner, c)).astype(bf16)
        to_b(1, c, far_inner).start()

    def middle(k, c):
        part = block((far_outer, far_inner)[k], c)
        to_a(k, c, near_inner).wait_recv()
        gps[k, c] = (part + gpa[k, c].astype(f32)).astype(bf16)
        to_b(k, c, far_inner).start()

    def back_to_end(c):
        part = block(near_outer, c)
        to_b(0, c, far_inner).wait_recv()
        gps[2, c] = (part + gpb[0, c].astype(f32)).astype(bf16)
        to_end(c, near_outer).start()

    def chunk_cols(c):
        return pl.ds(pl.multiple_of(c * wide, wide), wide)

    def own_block(c):
        gp_ref[:, chunk_cols(c)] = block(z, c)

    @pl.when(t != early)
    def _():
        cot_on(early, o).wait_recv()

    @pl.when(t == early)
    def _():
        cot_land(1 - early)

    for i in range(2):
        remote(ct.at[2 * t + i, 0], ct.at[2 * o + i, 0], co_s.at[i], co_r.at[i], s, o).wait_recv()

    def far_inner_ready():
        @pl.when(t != early)
        def _():
            cot_on(1 - early, o).wait_recv()

    def back_first():
        gh_land()
        back_other(0, tiles)
        b_side.start()

    def own_blocks():
        for c in range(chunks):
            own_block(c)

    def back_last():
        b_side.wait_recv()
        back_own(0, tiles)

    rest = list(range(ahead, chunks))

    gh_send()

    @pl.when(outer)
    def _():
        last_parts()
        act_land(0)
        feed(0, 0)
        mixed_other()
        far_inner_ready()
        for c in range(1, chunks):
            act_land(c)
            feed(0, c)
            if c - 1 in rest:
                feed(1, c - 1)
            if c == 1:
                mixed_own()
        feed(1, chunks - 1)
        cot_land_late(next_one)
        cot_land_late_on(next_one)
        for c in rest:
            feed(2, c)
        cot_land_late(last_one)
        cot_land_late_on(last_one)
        own_blocks()
        back_first()
        back_last()

    @pl.when(inner)
    def _():
        mixed_other()
        far_inner_ready()
        if ahead:
            ahead_land()
        mixed_own()
        act_ahead_land()
        last_parts()
        cot_land_late(next_one)
        act_land(0)
        middle(0, 0)
        cot_land_late_on(next_one)
        for c in range(1, chunks):
            act_land(c)
            middle(0, c)
            if c - 1 in rest:
                middle(1, c - 1)
            if c > 1:
                back_to_end(c - 2)
        back_first()
        back_to_end(chunks - 2)
        back_to_end(chunks - 1)
        middle(1, chunks - 1)
        if ahead:
            ahead_land_on()
            for c in range(ahead):
                middle_ahead(c)
        cot_land_late(last_one)
        cot_land_late_on(last_one)
        own_blocks()
        for c in range(ahead):
            gp_ref[:, chunk_cols(c)] += block_ahead(z, c)
        back_last()

    for c in range(chunks):
        @pl.when(outer)
        def _():
            to_end(c, near_outer).wait_recv()
            gp_ref[:, chunk_cols(c)] += gpa[0, c].astype(f32)

        @pl.when(inner)
        def _():
            to_b(1, c, far_inner).wait_recv()
            part = gp_ref[:, chunk_cols(c)] + gpb[1, c].astype(f32)
            if c >= ahead:
                to_a(2, c, near_inner).wait_recv()
                part += gpa[2, c].astype(f32)
            gp_ref[:, chunk_cols(c)] = part

    when_low(to_low.wait_send)
    when_high(to_high.wait_send)
    when_low(rim_on(0).wait_send)
    when_high(rim_on(1).wait_send)
    when_low(gh_low.wait_send)
    when_high(gh_high.wait_send)
    for copy in [x_side, d_side, m_side, b_side] + cot_own:
        copy.wait_send()
    for i in range(2):
        cot_pair(i).wait_send()
        cot_on(i, t).wait_send()
    for c in range(chunks):
        for copy in act_copies(c):
            copy.wait_send()
        if c >= ahead:
            for k in range(3):
                to_a(k, c, near_inner).wait_send()

    @pl.when(sends_ahead)
    def _():
        for side in range(2):
            cot_ahead(mine_ahead, side).wait_send()
        for c in range(ahead):
            act_ahead(c).wait_send()
            to_a(0, c, near_inner).wait_send()

    @pl.when(takes_ahead)
    def _():
        for side in range(2):
            cot_ahead_on(mine_ahead, side, t).wait_send()
        for c in range(ahead):
            act_ahead_on(c).wait_send()
            for k in range(3):
                to_a(k, c, near_inner).wait_send()


def writer(out_ref, gi_ref, gp_ref, out_hbm, gi_hbm, gp_hbm, sem):
    copies = [
        pltpu.make_async_copy(src, dst, sem.at[i])
        for i, (src, dst) in enumerate(
            ((gp_ref, gp_hbm), (out_ref, out_hbm), (gi_ref, gi_hbm))
        )
    ]
    for copy in copies:
        copy.start()
    for copy in copies:
        copy.wait()


def local8(inputs, w_dilated, w_point, cotangent):
    T, H = inputs.shape
    C = w_point.shape[0]
    R = DILATION_BINS
    tile, wide, ahead = 256, 128, 0
    tiles, chunks = H // tile, H // wide
    rows = C // 8
    bf16, f32 = jnp.bfloat16, jnp.float32
    dma = pltpu.SemaphoreType.DMA
    vmem = pl.BlockSpec(memory_space=pltpu.VMEM)
    hbm = pl.BlockSpec(memory_space=pltpu.HBM)
    shapes = [
        ((3, C, H), bf16), ((C, H), bf16), ((2, T + 2 * R, H), bf16), ((2, 2, R, H), bf16),
        ((T, H), f32), ((T, H), f32), ((chunks, T, wide), bf16), ((chunks, T, wide), bf16),
        ((2, T, H), bf16), ((H, T), bf16), ((4, 2, rows, T), bf16), ((T + 2 * R, H), bf16),
        ((T, H), bf16), ((T, H), bf16), ((T, H), bf16), ((T, H), bf16),
        ((3, chunks, rows, wide), bf16), ((3, chunks, rows, wide), bf16),
        ((2, chunks, rows, wide), bf16),
    ]
    one = dma(())
    two = dma((2,))
    sems = [
        dma((9,)), one, one, one, one, two, two, two, two, two, two,
        two, two, two, two, dma((chunks,)), dma((chunks,)), two, two, one, one, one, one,
        dma((3, chunks)), dma((3, chunks)), dma((2, chunks)),
    ]
    held = max(ahead, 1)
    late = [
        ((4, 2, rows, T), bf16), ((2, held, T, wide), bf16),
    ]
    late_sems = [
        dma((tile // wide, 3)), dma((tile // wide, 3)), dma((2, 2)), dma((2, 2)), dma((2, 2)),
        dma((2, 2)), dma((held,)), dma((held,)), dma((held,)), dma((held,)),
    ]
    outs = [
        jax.ShapeDtypeStruct((T, H), bf16),
        jax.ShapeDtypeStruct((T, H), bf16),
        jax.ShapeDtypeStruct((rows, H), f32),
    ]
    results = pl.pallas_call(
        functools.partial(kernel8, tile, ahead),
        out_shape=[pltpu.VMEM(out.shape, out.dtype) for out in outs],
        in_specs=[hbm] * 4,
        out_specs=[vmem] * 3,
        scratch_shapes=[pltpu.VMEM(*shape) for shape in shapes] + sems
        + [pltpu.VMEM(*shape) for shape in late] + late_sems,
        compiler_params=pltpu.CompilerParams(
            collective_id=0, has_side_effects=True, vmem_limit_bytes=60 * 1024 * 1024
        ),
    )(inputs, jnp.transpose(w_dilated, (1, 0, 2)), w_point, cotangent)
    return tuple(
        pl.pallas_call(
            writer,
            out_shape=outs,
            in_specs=[vmem] * 3,
            out_specs=[hbm] * 3,
            scratch_shapes=[dma((3,))],
            compiler_params=pltpu.CompilerParams(vmem_limit_bytes=1024 * 1024),
        )(*results)
    )


def local(n, inputs, w_dilated, w_point, cotangent):
    if n == 8 and inputs.shape[0] == 256:
        return local8(inputs, w_dilated, w_point, cotangent)
    T, H = inputs.shape
    C = w_point.shape[0]
    R = DILATION_BINS
    tile = 256
    tiles = H // tile
    rows = C // n
    bf16, f32 = jnp.bfloat16, jnp.float32
    with_point = rows % 16 == 0 and n % 2 == 0
    nz = n // 2
    vmem = pl.BlockSpec(memory_space=pltpu.VMEM)
    hbm = pl.BlockSpec(memory_space=pl.ANY)
    plane = jax.ShapeDtypeStruct((T, H), bf16)
    act_shape = (tiles, T, tile)
    outs = [plane, plane]
    scratch = []
    if with_point:
        outs += [jax.ShapeDtypeStruct((rows, H), f32)]
        scratch += [pltpu.VMEM(act_shape, bf16), pltpu.VMEM((T, C), bf16)]
    else:
        outs += [jax.ShapeDtypeStruct(act_shape, bf16), jax.ShapeDtypeStruct((T, C), bf16)]
    dma = pltpu.SemaphoreType.DMA
    scratch += [
        pltpu.VMEM((3, C, H), bf16),
        pltpu.VMEM((C, H), bf16),
        pltpu.VMEM((T + 2 * R, C), bf16),
        pltpu.VMEM((T, H), f32),
        pltpu.VMEM((T + 2 * R, H), bf16),
        pltpu.VMEM((T, H), bf16),
        pltpu.VMEM((T, H), bf16),
        pltpu.VMEM((T, H), bf16),
        pltpu.VMEM((T, H), bf16),
        dma((4,)), dma((6,)), dma((6,)), dma((4,)), dma((4,)), dma((2,)), dma((2,)),
    ]
    if with_point:
        scratch += [
            pltpu.VMEM(act_shape, bf16),
            pltpu.VMEM((T, H), bf16),
            pltpu.VMEM((T, H), bf16),
            pltpu.VMEM((C, 2 * T), bf16),
            pltpu.VMEM((nz - 1, tiles, rows, tile), bf16),
            pltpu.VMEM((nz - 1, tiles, rows, tile), bf16),
            dma((tiles,)), dma((tiles,)), dma((nz - 1, tiles)), dma((nz - 1, tiles)),
        ]
    results = pl.pallas_call(
        functools.partial(kernel, n, tile, with_point),
        out_shape=outs,
        in_specs=[vmem, hbm, hbm, vmem],
        out_specs=[vmem] * len(outs),
        scratch_shapes=scratch,
        compiler_params=pltpu.CompilerParams(
            collective_id=0, has_side_effects=True, vmem_limit_bytes=48 * 1024 * 1024
        ),
    )(inputs, jnp.transpose(w_dilated, (1, 0, 2)), w_point, cotangent)
    if with_point:
        return tuple(results)
    output, grad_inputs, act, full_grad = results
    activation = jnp.transpose(act, (1, 0, 2)).reshape(T, H)
    grad_point = lax.psum_scatter(
        jnp.einsum("to,tc->oc", full_grad, activation, preferred_element_type=f32),
        "seq",
        scatter_dimension=0,
        tiled=True,
    )
    return (output, grad_inputs, grad_point)


def solution(mesh):
    placed = (
        P(("groups", "seq"), "tensor"),
        P(None, None, "tensor"),
        P(None, "tensor"),
        P(("groups", "seq"), "tensor"),
    )
    return jax.shard_map(
        functools.partial(local, mesh.shape["seq"]),
        mesh=mesh,
        in_specs=placed,
        out_specs=(
            P(("groups", "seq"), "tensor"),
            P(("groups", "seq"), "tensor"),
            P(("groups", "seq"), "tensor"),
        ),
        check_vma=False,
    )
```
